128 devices in a mesh: subj: 32 (over z, y, core), vox: 4 (over x).
Axes of the slice: x: 4, y: 4, z: 4, core: 2. Of those that a mesh axis runs over, the one named last changes fastest.
Arguments:
- scans: bfloat16 [20480, 49152], P('subj', 'vox'), may hold values from -6 to 6
- test_matrix: bfloat16 [49152, 128], P('vox'), may hold values from -6 to 6
- lengths: int32 [32], replicated, may hold values from 160 to 640, as said below
- block_subject: int32 [32], replicated, may hold values from 0 to 31, each once
Outputs:
- basis: float32 [49152, 128], P('vox')
The draws below stay inside these ranges and needn't reach their ends.
Inputs may be any that keep to these rules, and one draw needn't show every extreme that they name: `lengths`: one subject has exactly 640 rows and one exactly 160. `block_subject`: each subject appears once.
All inputs are finite; a program needn't handle non-finite values.
Results may differ from the reference program's by a relative error of at most 0.0046.
Values may be sent and summed in bfloat16 or wider, within the bound.
A program may use at most 128 MiB of HBM per device.

```python
import jax
import jax.numpy as jnp
from jax import lax

V = 49152
R = 128
TPAD = 640
PASSES = 2
SUBJECTS = 32


def draw_lengths(key, part):
    first_key, second_key = jax.random.split(jax.random.fold_in(key, 17))
    values = jax.random.randint(first_key, (SUBJECTS,), TPAD // 4, TPAD + 1)
    order_ids = jax.random.permutation(second_key, SUBJECTS)
    values = values.at[order_ids[0]].set(TPAD)
    values = values.at[order_ids[1]].set(TPAD // 4)
    return values.astype(jnp.int32)


def draw_scans(key, part):
    keys = jax.random.split(jax.random.fold_in(key, 29), 5)
    row_total = SUBJECTS * TPAD
    first_time = jax.random.truncated_normal(keys[1], -3.0, 3.0, (row_total, 1), jnp.float32)
    second_time = jax.random.truncated_normal(keys[2], -3.0, 3.0, (row_total, 1), jnp.float32)
    first_space = jax.random.rademacher(keys[3], (1, V), dtype=jnp.float32)
    second_space = jax.random.rademacher(keys[4], (1, V), dtype=jnp.float32)
    half_mask = (jnp.arange(V, dtype=jnp.int32) >= V // 2).astype(jnp.float32)[None, :]
    noise = jax.random.truncated_normal(keys[0], -4.0, 4.0, (row_total, V), jnp.float32)
    first_amp = 0.2
    second_amp = 0.25
    values = noise + first_amp * first_time * first_space + second_amp * second_time * second_space * half_mask
    return values.astype(jnp.bfloat16)


def block_levels(own_key, shape, cuts, smallest, top_value):
    loudness = 1.0
    for position, blocks in cuts:
        steps = jax.random.uniform(jax.random.fold_in(jax.random.fold_in(own_key, 6), position), (blocks,), jnp.float32, smallest / len(cuts), top_value / len(cuts))
        loudness = loudness * jnp.repeat(jnp.exp(steps), shape[position] // blocks).reshape((-1,) + (1,) * (len(shape) - 1 - position))
    return loudness


def normal_values(stream_key, shape, spread, reach, cuts=(), held_as=jnp.bfloat16):
    result = spread * jax.random.normal(stream_key, shape, jnp.float32)
    if cuts:
        result = result * block_levels(stream_key, shape, cuts, -0.22, 0.18)
    return jnp.clip(result, -reach, reach).astype(held_as)


def setup_inputs(seed: int = 0) -> dict:
    streams_of = jax.random.split(jax.random.key(seed), 5)
    return {
        "scans": draw_scans(jax.random.fold_in(streams_of[4], 71), 0),
        "test_matrix": normal_values(streams_of[1], (V, R), 1.0, 6.0, ((0, 4),)),
        "lengths": draw_lengths(jax.random.fold_in(streams_of[4], 71), 0),
        "block_subject": jax.random.permutation(streams_of[3], SUBJECTS).astype(jnp.int32),
    }


def reference(scans, test_matrix, lengths, block_subject):
    blocks = scans.reshape(SUBJECTS, TPAD, V)
    live_len = lengths[block_subject].astype(jnp.int32)
    time_ids = jnp.arange(TPAD, dtype=jnp.int32)
    panel_now = test_matrix
    orthonormal = jnp.zeros((V, R), jnp.float32)
    for sweep_index in range(PASSES):

        def add_subject(running, inputs):
            data_block, length = inputs
            scores = jnp.dot(data_block.astype(jnp.float32), panel_now.astype(jnp.float32), preferred_element_type=jnp.float32)
            scores = jnp.where((time_ids < length)[:, None], scores, jnp.float32(0.0)).astype(jnp.bfloat16)
            update = lax.dot_general(data_block.astype(jnp.float32), scores.astype(jnp.float32), (((0,), (0,)), ((), ())), preferred_element_type=jnp.float32)
            return (running + update, None)
        sketch, unused = lax.scan(add_subject, jnp.zeros((V, R), jnp.float32), (blocks, live_len))
        gram_matrix = jnp.dot(sketch.T, sketch, precision=lax.Precision.HIGHEST) / V
        factor = jnp.linalg.cholesky(gram_matrix)
        orthonormal = jax.scipy.linalg.solve_triangular(factor, sketch.T, lower=True).T
        panel_now = orthonormal.astype(jnp.bfloat16)
    return orthonormal
```

```python
import functools

import jax
import jax.numpy as jnp
from jax import lax
from jax.experimental import pallas as pl
from jax.experimental.pallas import tpu as pltpu
from jax.sharding import PartitionSpec as P

V = 49152
PASSES = 2
MESH = pl.DeviceIdType.MESH
VMEM_BYTES = 60 * 2**20
ANY = pl.BlockSpec(memory_space=pl.ANY)
VMEM = pl.BlockSpec(memory_space=pltpu.VMEM)
SMEM = pl.BlockSpec(memory_space=pltpu.SMEM)
ORDERS = (("ya", "yb", "za", "zb"), ("yb", "ya", "zb", "za"), ("za", "zb", "ya", "yb"), ("zb", "za", "yb", "ya"))


def ring_bits(i):
    b = lax.div(i, 2)
    return lax.rem(i + b, 2), b


def flip_a(i):
    return i + 1 - 2 * lax.rem(i, 2)


def flip_b(i):
    return 3 - i


class Place:
    def __init__(self):
        here = lax.axis_index("subj")
        self.z, self.y, self.c = lax.div(here, 8), lax.rem(lax.div(here, 2), 4), lax.rem(here, 2)
        self.x = lax.axis_index("vox")
        self.bits = place_bits(self.z, self.y)

    def sibling(self):
        return {"subj": self.z * 8 + self.y * 2 + 1 - self.c}

    def across(self, bit):
        z, y = self.z, self.y
        if bit[0] == "x":
            return {"vox": flip_a(self.x) if bit == "xa" else flip_b(self.x)}
        if bit[0] == "y":
            y = flip_a(y) if bit == "ya" else flip_b(y)
        else:
            z = flip_a(z) if bit == "za" else flip_b(z)
        return {"subj": z * 8 + y * 2 + self.c}


def place_bits(z, y):
    ya, yb = ring_bits(y)
    za, zb = ring_bits(z)
    return {"ya": ya, "yb": yb, "za": za, "zb": zb}


def index_in(order, bits):
    return 8 * bits[order[0]] + 4 * bits[order[1]] + 2 * bits[order[2]] + bits[order[3]]


def meet(devices):
    barrier = pltpu.get_barrier_semaphore()
    for device in devices:
        pl.semaphore_signal(barrier, inc=1, device_id=device, device_id_type=MESH)
    pl.semaphore_wait(barrier, len(devices))


def send(src, dst, send_sem, recv_sem, device):
    copy = pltpu.make_async_remote_copy(
        src_ref=src, dst_ref=dst, send_sem=send_sem, recv_sem=recv_sem, device_id=device, device_id_type=MESH
    )
    copy.start()
    return copy


def scores_kernel(lengths, block_subject, scans, panel, out, held, part, got, full, load_sem, s1, r1, s2, r2):
    x = lax.axis_index("vox")
    rows = part.shape[1]
    depth = panel.shape[0]
    owners = [lax.rem(x + step, 4) for step in (2, 1, 3, 0)]
    loads = []
    for t in range(4):
        start = pl.multiple_of(owners[t] * rows, rows)
        loads.append(pltpu.make_async_copy(scans.at[pl.ds(start, rows)], held.at[t], load_sem.at[t]))
        loads[t].start()
    meet([{"vox": owners[t]} for t in range(3)])
    tile = 3072
    copies = []
    for t in range(4):
        loads[t].wait()

        def add(k, acc, t=t):
            at = pl.multiple_of(k * tile, tile)
            return acc + jnp.dot(
                held[t, :, pl.ds(at, tile)], panel[pl.ds(at, tile), :], preferred_element_type=jnp.float32
            )

        part[t] = lax.fori_loop(0, depth // tile, add, jnp.zeros(part.shape[1:], jnp.float32))
        if t < 3:
            copies.append(send(part.at[t], got.at[t], s1.at[t], r1.at[t], {"vox": owners[t]}))
    total = part[3]
    for t in range(3):
        copies[t].wait()
        total = total + got[t]
    length = lengths[block_subject[lax.axis_index("subj")]]
    time_ids = x * rows + lax.broadcasted_iota(jnp.int32, total.shape, 0)
    full[x] = jnp.where(time_ids < length, total, jnp.float32(0.0)).astype(jnp.bfloat16)
    copies = [send(full.at[x], full.at[x], s2.at[t], r2.at[t], {"vox": owners[t]}) for t in range(3)]
    for copy in copies:
        copy.wait()
    for i in range(4):
        out[pl.ds(i * rows, rows), :] = full[i]


def scores_call(lengths, block_subject, scans, panel, number):
    time_rows, cols = scans.shape
    rank = panel.shape[1]
    rows = time_rows // 4
    return pl.pallas_call(
        scores_kernel,
        out_shape=jax.ShapeDtypeStruct((time_rows, rank), jnp.bfloat16),
        in_specs=[SMEM, SMEM, ANY, VMEM],
        out_specs=VMEM,
        scratch_shapes=[
            pltpu.VMEM((4, rows, cols), jnp.bfloat16),
            pltpu.VMEM((4, rows, rank), jnp.float32),
            pltpu.VMEM((3, rows, rank), jnp.float32),
            pltpu.VMEM((4, rows, rank), jnp.bfloat16),
            pltpu.SemaphoreType.DMA((4,)),
            pltpu.SemaphoreType.DMA((3,)),
            pltpu.SemaphoreType.DMA((3,)),
            pltpu.SemaphoreType.DMA((3,)),
            pltpu.SemaphoreType.DMA((3,)),
        ],
        compiler_params=pltpu.CompilerParams(
            collective_id=number, has_side_effects=True, vmem_limit_bytes=VMEM_BYTES
        ),
        name=f"scores_{number}",
    )(lengths, block_subject, scans, panel)


def sketch_kernel(
    scans, scores, z_out, g_out, held, away, arrived, mine, in1, in2, in3, in4, g_part, g_in, g_sum, g_last,
    load_sem, sc, rc, ss, rs, sg, rg,
):
    place = Place()
    width = held.shape[2]
    rank, piece = z_out.shape
    quarter = rank // 4
    slots = held.shape[0]

    def block_of(t):
        core = lax.rem(place.c + 1 + t // 4, 2)
        return core * 16 + (t % 4) * 4

    def load(t):
        start = pl.multiple_of(block_of(t) * piece, width)
        return pltpu.make_async_copy(scans.at[:, pl.ds(start, width)], held.at[t % slots], load_sem.at[t % slots])

    for t in range(slots - 1):
        load(t).start()
    bits7 = ("xa", "xb", "ya", "yb", "za", "zb")
    meet([place.sibling()] + [place.across(bit) for bit in bits7])
    left = scores[...].T
    core_copies = []
    for t in range(8):
        if t + slots - 1 < 8:
            load(t + slots - 1).start()
        load(t).wait()
        z = t % 4
        block = jnp.dot(left, held[t % slots], preferred_element_type=jnp.float32)
        if t >= 4:
            core_copies[z].wait()
        for y in range(4):
            bits = place_bits(jnp.int32(z), jnp.int32(y))
            for q in range(4):
                value = block[q * quarter : (q + 1) * quarter, y * piece : (y + 1) * piece]
                if t < 4:
                    away[z, q, y] = value
                else:
                    mine[q, static_index(ORDERS[q], z, y)] = value + arrived[z, q, y]
        if t < 4:
            core_copies.append(send(away.at[z], arrived.at[z], sc.at[z], rc.at[z], place.sibling()))

    offset = [jnp.int32(0)] * 4
    for stage, inbox in enumerate((in1, in2, in3, in4)):
        half = 8 >> stage
        copies = []
        for q in range(4):
            bit = ORDERS[q][stage]
            there = offset[q] + (1 - place.bits[bit]) * half
            n = stage * 4 + q
            copies.append(
                send(mine.at[q, pl.ds(there, half)], inbox.at[q], ss.at[n], rs.at[n], place.across(bit))
            )
            offset[q] = offset[q] + place.bits[bit] * half
        for q in range(4):
            copies[q].wait()

            def add(i, carry, q=q, inbox=inbox):
                at = offset[q] + i
                mine[q, at] = mine[q, at] + inbox[q, i]
                return carry

            lax.fori_loop(0, half, add, 0)
    for q in range(4):
        z_out[pl.ds(q * quarter, quarter), :] = mine[q, offset[q]]

    own = z_out[...]
    gram = lax.dot_general(
        own, own, (((1,), (1,)), ((), ())), precision=lax.Precision.HIGHEST, preferred_element_type=jnp.float32
    )
    rows = rank // 2
    g_part[0] = gram[:rows]
    g_part[1] = gram[rows:]
    copy = send(g_part.at[1 - place.c], g_in.at[0], sg.at[0], rg.at[0], place.sibling())
    copy.wait()
    g_sum[0] = g_part[place.c] + g_in[0]
    for n, bit in enumerate(bits7):
        copy = send(g_sum.at[n], g_in.at[n + 1], sg.at[n + 1], rg.at[n + 1], place.across(bit))
        copy.wait()
        g_sum[n + 1] = g_sum[n] + g_in[n + 1]
    g_last[place.c] = g_sum[6]
    copy = send(g_last.at[place.c], g_last.at[place.c], sg.at[7], rg.at[7], place.sibling())
    copy.wait()
    g_out[pl.ds(0, rows), :] = g_last[0]
    g_out[pl.ds(rows, rows), :] = g_last[1]


def static_index(order, z, y):
    bits = {"ya": (y + y // 2) % 2, "yb": y // 2, "za": (z + z // 2) % 2, "zb": z // 2}
    return index_in(order, bits)


def sketch_call(scans, scores, number):
    time_rows, cols = scans.shape
    rank = scores.shape[1]
    piece = cols // 32
    f32 = jnp.float32
    quarter = rank // 4
    return pl.pallas_call(
        sketch_kernel,
        out_shape=(jax.ShapeDtypeStruct((rank, piece), f32), jax.ShapeDtypeStruct((rank, rank), f32)),
        in_specs=[ANY, VMEM],
        out_specs=(VMEM, VMEM),
        scratch_shapes=[
            pltpu.VMEM((4, time_rows, 4 * piece), jnp.bfloat16),
            pltpu.VMEM((4, 4, 4, quarter, piece), f32),
            pltpu.VMEM((4, 4, 4, quarter, piece), f32),
            pltpu.VMEM((4, 16, quarter, piece), f32),
            pltpu.VMEM((4, 8, quarter, piece), f32),
            pltpu.VMEM((4, 4, quarter, piece), f32),
            pltpu.VMEM((4, 2, quarter, piece), f32),
            pltpu.VMEM((4, 1, quarter, piece), f32),
            pltpu.VMEM((2, rank // 2, rank), f32),
            pltpu.VMEM((7, rank // 2, rank), f32),
            pltpu.VMEM((7, rank // 2, rank), f32),
            pltpu.VMEM((2, rank // 2, rank), f32),
            pltpu.SemaphoreType.DMA((4,)),
            pltpu.SemaphoreType.DMA((4,)),
            pltpu.SemaphoreType.DMA((4,)),
            pltpu.SemaphoreType.DMA((16,)),
            pltpu.SemaphoreType.DMA((16,)),
            pltpu.SemaphoreType.DMA((8,)),
            pltpu.SemaphoreType.DMA((8,)),
        ],
        compiler_params=pltpu.CompilerParams(
            collective_id=number, has_side_effects=True, vmem_limit_bytes=VMEM_BYTES
        ),
        name=f"sketch_{number}",
    )(scans, scores)


def gather_kernel(slice_t, out, pieces, ss, rs, sc, rc):
    place = Place()
    size = pieces.shape[3]
    bits4 = ("ya", "yb", "za", "zb")
    meet([place.sibling()] + [place.across(bit) for bit in bits4])
    own = slice_t[...].T.astype(jnp.bfloat16)
    index = [index_in(ORDERS[q], place.bits) for q in range(4)]
    for q in range(4):
        pieces[q, place.c, index[q]] = own[q * size : (q + 1) * size]
    pending = []

    def to_sibling(q, start, count, n):
        ref = pieces.at[q, place.c, pl.ds(start, count)]
        pending.append(send(ref, ref, sc.at[n * 4 + q], rc.at[n * 4 + q], place.sibling()))

    for stage in range(4):
        count = 1 << stage
        copies = []
        for q in range(4):
            bit = ORDERS[q][3 - stage]
            start = lax.div(index[q], count) * count
            ref = pieces.at[q, place.c, pl.ds(start, count)]
            n = stage * 4 + q
            copies.append(send(ref, ref, ss.at[n], rs.at[n], place.across(bit)))
        for q in range(4):
            if stage == 0:
                to_sibling(q, index[q], 1, 0)
        for q in range(4):
            copies[q].wait()
            bit = ORDERS[q][3 - stage]
            base = lax.div(index[q], 2 * count) * (2 * count)
            to_sibling(q, base + (1 - place.bits[bit]) * count, count, stage + 1)
    for copy in pending:
        copy.wait()

    def put(n, carry):
        core, zy = lax.div(n, 16), lax.rem(n, 16)
        bits = place_bits(lax.div(zy, 4), lax.rem(zy, 4))
        for q in range(4):
            at = pl.multiple_of(n * (4 * size) + q * size, 16)
            out[pl.ds(at, size), :] = pieces[q, core, index_in(ORDERS[q], bits)]
        return carry

    lax.fori_loop(0, 32, put, 0)


def gather_call(slice_t, number):
    rank, piece = slice_t.shape
    return pl.pallas_call(
        gather_kernel,
        out_shape=jax.ShapeDtypeStruct((32 * piece, rank), jnp.bfloat16),
        in_specs=[VMEM],
        out_specs=VMEM,
        scratch_shapes=[
            pltpu.VMEM((4, 2, 16, piece // 4, rank), jnp.bfloat16),
            pltpu.SemaphoreType.DMA((16,)),
            pltpu.SemaphoreType.DMA((16,)),
            pltpu.SemaphoreType.DMA((20,)),
            pltpu.SemaphoreType.DMA((20,)),
        ],
        compiler_params=pltpu.CompilerParams(
            collective_id=number, has_side_effects=True, vmem_limit_bytes=VMEM_BYTES
        ),
        name=f"gather_{number}",
    )(slice_t)


def on_device(scans, test_matrix, lengths, block_subject):
    panel = test_matrix
    for sweep in range(PASSES):
        scores = scores_call(lengths, block_subject, scans, panel, 3 * sweep)
        slice_t, gram = sketch_call(scans, scores, 3 * sweep + 1)
        factor = jnp.linalg.cholesky(gram / V)
        orthonormal_t = jax.scipy.linalg.solve_triangular(factor, slice_t, lower=True)
        panel = gather_call(orthonormal_t, 3 * sweep + 2)
    return panel.astype(jnp.float32)


def solution(mesh):
    placed = (P("subj", "vox"), P("vox", None), P(), P())
    return jax.shard_map(
        on_device, mesh=mesh, in_specs=placed, out_specs=P("vox", None), check_vma=False
    )
```

```python
import functools

import jax
import jax.numpy as jnp
from jax import lax
from jax.experimental import pallas as pl
from jax.experimental.pallas import tpu as pltpu
from jax.sharding import PartitionSpec as P

V = 49152
PASSES = 2
MESH = pl.DeviceIdType.MESH
VMEM_BYTES = 60 * 2**20
ANY = pl.BlockSpec(memory_space=pl.ANY)
VMEM = pl.BlockSpec(memory_space=pltpu.VMEM)
SMEM = pl.BlockSpec(memory_space=pltpu.SMEM)
ORDERS = (("ya", "yb", "za", "zb"), ("yb", "ya", "zb", "za"), ("za", "zb", "ya", "yb"), ("zb", "za", "yb", "ya"))


def ring_bits(i):
    b = i // 2 if isinstance(i, int) else lax.div(i, 2)
    return (i + b) % 2 if isinstance(i, int) else lax.rem(i + b, 2), b


def flip_a(i):
    return i + 1 - 2 * lax.rem(i, 2)


def flip_b(i):
    return 3 - i


class Place:
    def __init__(self):
        here = lax.axis_index("subj")
        self.z, self.y, self.c = lax.div(here, 8), lax.rem(lax.div(here, 2), 4), lax.rem(here, 2)
        self.x = lax.axis_index("vox")
        self.bits = place_bits(self.z, self.y)

    def sibling(self):
        return {"subj": self.z * 8 + self.y * 2 + 1 - self.c}

    def across(self, bit):
        z, y = self.z, self.y
        if bit[0] == "x":
            return {"vox": flip_a(self.x) if bit == "xa" else flip_b(self.x)}
        if bit[0] == "y":
            y = flip_a(y) if bit == "ya" else flip_b(y)
        else:
            z = flip_a(z) if bit == "za" else flip_b(z)
        return {"subj": z * 8 + y * 2 + self.c}


def place_bits(z, y):
    ya, yb = ring_bits(y)
    za, zb = ring_bits(z)
    return {"ya": ya, "yb": yb, "za": za, "zb": zb}


def index_in(order, bits):
    return 8 * bits[order[0]] + 4 * bits[order[1]] + 2 * bits[order[2]] + bits[order[3]]


def greet(devices):
    barrier = pltpu.get_barrier_semaphore()
    for device in devices:
        pl.semaphore_signal(barrier, inc=1, device_id=device, device_id_type=MESH)
    return barrier, len(devices)


def meet(devices):
    pl.semaphore_wait(*greet(devices))


def send(src, dst, send_sem, recv_sem, device):
    copy = pltpu.make_async_remote_copy(
        src_ref=src, dst_ref=dst, send_sem=send_sem, recv_sem=recv_sem, device_id=device, device_id_type=MESH
    )
    copy.start()
    return copy


def scores_kernel(lengths, block_subject, scans, panel, out, held, part, got, full, load_sem, s1, r1, s2, r2):
    x = lax.axis_index("vox")
    rows = part.shape[1]
    depth = panel.shape[0]
    owners = [lax.rem(x + step, 4) for step in (2, 1, 3, 0)]
    loads = []
    for t in range(4):
        start = pl.multiple_of(owners[t] * rows, rows)
        loads.append(pltpu.make_async_copy(scans.at[pl.ds(start, rows)], held.at[t], load_sem.at[t]))
        loads[t].start()
    meet([{"vox": owners[t]} for t in range(3)])
    tile = 3072
    copies = []
    for t in range(4):
        loads[t].wait()

        def add(k, acc, t=t):
            at = pl.multiple_of(k * tile, tile)
            return acc + jnp.dot(
                held[t, :, pl.ds(at, tile)], panel[pl.ds(at, tile), :], preferred_element_type=jnp.float32
            )

        part[t] = lax.fori_loop(0, depth // tile, add, jnp.zeros(part.shape[1:], jnp.float32))
        if t < 3:
            copies.append(send(part.at[t], got.at[t], s1.at[t], r1.at[t], {"vox": owners[t]}))
    total = part[3]
    for t in range(3):
        copies[t].wait()
        total = total + got[t]
    length = lengths[block_subject[lax.axis_index("subj")]]
    time_ids = x * rows + lax.broadcasted_iota(jnp.int32, total.shape, 0)
    full[x] = jnp.where(time_ids < length, total, jnp.float32(0.0)).astype(jnp.bfloat16)
    copies = [send(full.at[x], full.at[x], s2.at[t], r2.at[t], {"vox": owners[t]}) for t in range(3)]
    for copy in copies:
        copy.wait()
    for i in range(4):
        out[pl.ds(i * rows, rows), :] = full[i]


def scores_call(lengths, block_subject, scans, panel, number):
    time_rows, cols = scans.shape
    rank = panel.shape[1]
    rows = time_rows // 4
    return pl.pallas_call(
        scores_kernel,
        out_shape=jax.ShapeDtypeStruct((time_rows, rank), jnp.bfloat16),
        in_specs=[SMEM, SMEM, ANY, VMEM],
        out_specs=VMEM,
        scratch_shapes=[
            pltpu.VMEM((4, rows, cols), jnp.bfloat16),
            pltpu.VMEM((4, rows, rank), jnp.float32),
            pltpu.VMEM((3, rows, rank), jnp.float32),
            pltpu.VMEM((4, rows, rank), jnp.bfloat16),
            pltpu.SemaphoreType.DMA((4,)),
            pltpu.SemaphoreType.DMA((3,)),
            pltpu.SemaphoreType.DMA((3,)),
            pltpu.SemaphoreType.DMA((3,)),
            pltpu.SemaphoreType.DMA((3,)),
        ],
        compiler_params=pltpu.CompilerParams(
            collective_id=number, has_side_effects=True, vmem_limit_bytes=VMEM_BYTES
        ),
        name=f"scores_{number}",
    )(lengths, block_subject, scans, panel)


def flipped(order, bits, m):
    index = 0
    for weight, bit in zip((8, 4, 2, 1), order):
        index = index + weight * (1 - bits[bit] if m & weight else bits[bit])
    return index


def sketch_kernel(
    scans, scores, z_out, g_out, held, away, arrived, mine, inbox, g_part, g_in, g_sum, g_last,
    load_sem, sc, rc, ss, rs, sg, rg,
):
    place = Place()
    width = held.shape[2]
    rank, piece = z_out.shape
    quarter = rank // 4
    slots = held.shape[0]
    z_far = (flip_a(flip_b(place.z)), flip_a(place.z), flip_b(place.z), place.z)
    z_flips = ({"za", "zb"}, {"za"}, {"zb"}, set())
    steps = [(1, 0), (1, 1), (0, 0), (1, 2), (0, 1), (1, 3), (0, 2), (0, 3)]

    def load(t):
        away_side, k = steps[t]
        core = 1 - place.c if away_side else place.c
        start = pl.multiple_of((core * 16 + z_far[k] * 4) * piece, width)
        return pltpu.make_async_copy(scans.at[:, pl.ds(start, width)], held.at[t % slots], load_sem.at[t % slots])

    for t in range(slots - 1):
        load(t).start()
    bits6 = ("xa", "xb", "ya", "yb", "za", "zb")
    meet([place.sibling()] + [place.across(bit) for bit in bits6])
    left = scores[...].T
    core_copies = {}
    copies = []
    at = [[flipped(ORDERS[q], place.bits, m) for m in range(16)] for q in range(4)]

    def pass_on(q, m):
        bit = ORDERS[q][{8: 0, 4: 1, 2: 2, 1: 3}[1 << (m.bit_length() - 1)]]
        copies.append(send(mine.at[q, at[q][m]], inbox.at[q, m], ss.at[q, m], rs.at[q, m], place.across(bit)))

    def take(q, m, weight):
        ref = inbox.at[q, weight | m]
        pltpu.make_async_copy(ref, ref, rs.at[q, weight | m]).wait()
        return inbox[q, weight | m]

    for t in range(8):
        if t + slots - 1 < 8:
            load(t + slots - 1).start()
        load(t).wait()
        away_side, k = steps[t]
        block = jnp.dot(left, held[t % slots], preferred_element_type=jnp.float32)
        if not away_side:
            core_copies[k].wait()
        for y in range(4):
            bits = place_bits(z_far[k], y)
            for q in range(4):
                value = block[q * quarter : (q + 1) * quarter, y * piece : (y + 1) * piece]
                if away_side:
                    away[k, q, y] = value
                else:
                    mine[q, index_in(ORDERS[q], bits)] = value + arrived[k, q, y]
        if away_side:
            core_copies[k] = send(away.at[k], arrived.at[k], sc.at[k], rc.at[k], place.sibling())
            continue
        for m in range(15, 7, -1):
            for q in range(4):
                flips = {bit for weight, bit in zip((8, 4, 2, 1), ORDERS[q]) if m & weight}
                if flips & {"za", "zb"} == z_flips[k]:
                    pass_on(q, m)

    for m in range(7, -1, -1):
        for q in range(4):
            value = mine[q, at[q][m]]
            for weight in (8, 4, 2, 1):
                if weight > m:
                    value = value + take(q, m, weight)
            if m:
                mine[q, at[q][m]] = value
                pass_on(q, m)
            else:
                z_out[q * quarter : (q + 1) * quarter, :] = value

    own = z_out[...]
    gram = lax.dot_general(
        own, own, (((1,), (1,)), ((), ())), precision=lax.Precision.HIGHEST, preferred_element_type=jnp.float32
    )
    rows = rank // 2
    g_part[0] = gram[:rows]
    g_part[1] = gram[rows:]
    copy = send(g_part.at[1 - place.c], g_in.at[0], sg.at[0], rg.at[0], place.sibling())
    for done in copies:
        done.wait_send()
    copy.wait()
    g_sum[0] = g_part[place.c] + g_in[0]
    for n, bit in enumerate(bits6):
        copy = send(g_sum.at[n], g_in.at[n + 1], sg.at[n + 1], rg.at[n + 1], place.across(bit))
        copy.wait()
        g_sum[n + 1] = g_sum[n] + g_in[n + 1]
    g_last[place.c] = g_sum[6]
    copy = send(g_last.at[place.c], g_last.at[place.c], sg.at[7], rg.at[7], place.sibling())
    copy.wait()
    g_out[pl.ds(0, rows), :] = g_last[0]
    g_out[pl.ds(rows, rows), :] = g_last[1]


def sketch_call(scans, scores, number):
    time_rows, cols = scans.shape
    rank = scores.shape[1]
    piece = cols // 32
    f32 = jnp.float32
    quarter = rank // 4
    return pl.pallas_call(
        sketch_kernel,
        out_shape=(jax.ShapeDtypeStruct((rank, piece), f32), jax.ShapeDtypeStruct((rank, rank), f32)),
        in_specs=[ANY, VMEM],
        out_specs=(VMEM, VMEM),
        scratch_shapes=[
            pltpu.VMEM((4, time_rows, 4 * piece), jnp.bfloat16),
            pltpu.VMEM((4, 4, 4, quarter, piece), f32),
            pltpu.VMEM((4, 4, 4, quarter, piece), f32),
            pltpu.VMEM((4, 16, quarter, piece), f32),
            pltpu.VMEM((4, 16, quarter, piece), f32),
            pltpu.VMEM((2, rank // 2, rank), f32),
            pltpu.VMEM((7, rank // 2, rank), f32),
            pltpu.VMEM((7, rank // 2, rank), f32),
            pltpu.VMEM((2, rank // 2, rank), f32),
            pltpu.SemaphoreType.DMA((4,)),
            pltpu.SemaphoreType.DMA((4,)),
            pltpu.SemaphoreType.DMA((4,)),
            pltpu.SemaphoreType.DMA((4, 16)),
            pltpu.SemaphoreType.DMA((4, 16)),
            pltpu.SemaphoreType.DMA((8,)),
            pltpu.SemaphoreType.DMA((8,)),
        ],
        compiler_params=pltpu.CompilerParams(
            collective_id=number, has_side_effects=True, vmem_limit_bytes=VMEM_BYTES
        ),
        name=f"sketch_{number}",
    )(scans, scores)


def inverse_factor(gram):
    n, width = gram.shape[0], 8
    row, col = (lax.broadcasted_iota(jnp.int32, (n, n), d) for d in (0, 1))
    left, right = gram, (row == col).astype(jnp.float32)
    place = lax.broadcasted_iota(jnp.int32, (width, n), 0)
    done = []
    for k in range(0, n, width):
        columns = [jnp.broadcast_to(left[:, k + j : k + j + 1], left.shape) for j in range(width)]
        heads, tails = [c[:width] for c in columns], [c[width:] for c in columns]
        left_head, right_head = left[:width], right[:width]
        left, right = left[width:], right[width:]
        pivots = jnp.zeros((width, n), jnp.float32)
        for j in range(width):
            pivot = heads[j][j : j + 1]
            over = 1.0 / pivot
            pivots = jnp.where(place == j, jnp.broadcast_to(pivot, (width, n)), pivots)
            head = jnp.where(place > j, heads[j] * over, 0.0)
            left_row, right_row = left_head[j : j + 1], right_head[j : j + 1]
            if k + width < n:
                tail = tails[j] * over
                left, right = left - tail * left_row, right - tail * right_row
            for i in range(j + 1, width):
                factor = heads[j][i : i + 1]
                heads[i] = heads[i] - head * factor
                if k + width < n:
                    tails[i] = tails[i] - tail * factor
            left_head, right_head = left_head - head * left_row, right_head - head * right_row
        done.append(right_head * lax.rsqrt(pivots))
    return jnp.concatenate(done, 0)


def gather_kernel(slice_t, gram, out, pieces, ss, rs, sc, rc):
    place = Place()
    size = pieces.shape[3]
    greeted = greet([place.sibling()] + [place.across(bit) for bit in ("ya", "yb", "za", "zb")])
    inverse = inverse_factor(gram[...] / V)
    own = jnp.dot(inverse, slice_t[...], precision=lax.Precision.HIGHEST, preferred_element_type=jnp.float32)
    own = own.T.astype(jnp.bfloat16)
    at = [[flipped(ORDERS[q], place.bits, m) for m in range(16)] for q in range(4)]
    for q in range(4):
        pieces[q, place.c, at[q][0]] = own[q * size : (q + 1) * size]
    pl.semaphore_wait(*greeted)
    copies = []

    def pass_on(q, m):
        ref = pieces.at[q, place.c, at[q][m]]
        for weight, bit in ((1, 3), (2, 2), (4, 1), (8, 0)):
            if weight > m:
                n = weight | m
                copies.append(send(ref, ref, ss.at[q, n], rs.at[q, n], place.across(ORDERS[q][bit])))

    def to_sibling(q, m):
        ref = pieces.at[q, place.c, at[q][m]]
        copies.append(send(ref, ref, sc.at[q, m], rc.at[q, m], place.sibling()))

    for m in (0, 1, 2, 4, 3, 5, 6, 7, 8, 9, 10, 12, 11, 13, 14, 15):
        for q in range(4):
            if m:
                ref = pieces.at[q, place.c, at[q][m]]
                pltpu.make_async_copy(ref, ref, rs.at[q, m]).wait()
            pass_on(q, m)
            to_sibling(q, m)
    for q in range(4):
        for m in range(16):
            ref = pieces.at[q, 1 - place.c, at[q][m]]
            pltpu.make_async_copy(ref, ref, rc.at[q, m]).wait()
    for copy in copies:
        copy.wait_send()

    def put(n, carry):
        core, zy = lax.div(n, 16), lax.rem(n, 16)
        bits = place_bits(lax.div(zy, 4), lax.rem(zy, 4))
        for q in range(4):
            start = pl.multiple_of(n * (4 * size) + q * size, 16)
            out[pl.ds(start, size), :] = pieces[q, core, index_in(ORDERS[q], bits)]
        return carry

    lax.fori_loop(0, 32, put, 0)


def gather_call(slice_t, gram, number):
    rank, piece = slice_t.shape
    return pl.pallas_call(
        gather_kernel,
        out_shape=jax.ShapeDtypeStruct((32 * piece, rank), jnp.bfloat16),
        in_specs=[VMEM, VMEM],
        out_specs=VMEM,
        scratch_shapes=[pltpu.VMEM((4, 2, 16, piece // 4, rank), jnp.bfloat16)]
        + [pltpu.SemaphoreType.DMA((4, 16))] * 4,
        compiler_params=pltpu.CompilerParams(
            collective_id=number, has_side_effects=True, vmem_limit_bytes=VMEM_BYTES
        ),
        name=f"gather_{number}",
    )(slice_t, gram)


def on_device(scans, test_matrix, lengths, block_subject):
    panel = test_matrix
    for sweep in range(PASSES):
        scores = scores_call(lengths, block_subject, scans, panel, 3 * sweep)
        slice_t, gram = sketch_call(scans, scores, 3 * sweep + 1)
        panel = gather_call(slice_t, gram, 3 * sweep + 2)
    return panel.astype(jnp.float32)


def solution(mesh):
    placed = (P("subj", "vox"), P("vox", None), P(), P())
    return jax.shard_map(
        on_device, mesh=mesh, in_specs=placed, out_specs=P("vox", None), check_vma=False
    )
```

```python
import functools

import jax
import jax.numpy as jnp
from jax import lax
from jax.experimental import pallas as pl
from jax.experimental.pallas import tpu as pltpu
from jax.sharding import PartitionSpec as P

V = 49152
PASSES = 2
MESH = pl.DeviceIdType.MESH
VMEM_BYTES = 62 * 2**20
ANY = pl.BlockSpec(memory_space=pl.ANY)
VMEM = pl.BlockSpec(memory_space=pltpu.VMEM)
SMEM = pl.BlockSpec(memory_space=pltpu.SMEM)
DMA = pltpu.SemaphoreType.DMA
f32, bf16 = jnp.float32, jnp.bfloat16
ORDERS = (("ya", "yb", "za", "zb"), ("yb", "ya", "zb", "za"), ("za", "zb", "ya", "yb"), ("zb", "za", "yb", "ya"))
WEIGHTS = (8, 4, 2, 1)


def flip_a(i):
    return i + 1 - 2 * lax.rem(i, 2)


def flip_b(i):
    return 3 - i


class Place:
    def __init__(self):
        here = lax.axis_index("subj")
        self.z, self.y, self.c = lax.div(here, 8), lax.rem(lax.div(here, 2), 4), lax.rem(here, 2)
        self.x = lax.axis_index("vox")

    def flipped(self, bits):
        z, y = self.z, self.y
        z = flip_a(z) if "za" in bits else z
        z = flip_b(z) if "zb" in bits else z
        y = flip_a(y) if "ya" in bits else y
        y = flip_b(y) if "yb" in bits else y
        return z, y

    def across(self, bit):
        z, y = self.flipped((bit,))
        return {"subj": z * 8 + y * 2 + self.c}

    def sibling(self):
        return {"subj": self.z * 8 + self.y * 2 + 1 - self.c}

    def in_plane(self, step):
        z, y = lax.rem(self.z + step // 4, 4), lax.rem(self.y + step % 4, 4)
        return z * 4 + y, {"subj": z * 8 + y * 2 + self.c}

    def along_x(self, step, other_core):
        x = lax.rem(self.x + step, 4)
        c = 1 - self.c if other_core else self.c
        return x * 2 + c, {"subj": self.z * 8 + self.y * 2 + c, "vox": x}


def flips_of(order, m):
    return tuple(bit for weight, bit in zip(WEIGHTS, order) if m & weight)


def pair_index(place, q, m):
    z, y = place.flipped(flips_of(ORDERS[q], m))
    return z * 4 + y


def greet(devices):
    barrier = pltpu.get_barrier_semaphore()
    for device in devices:
        pl.semaphore_signal(barrier, inc=1, device_id=device, device_id_type=MESH)
    return barrier, len(devices)


def send(src, dst, send_sem, recv_sem, device):
    copy = pltpu.make_async_remote_copy(
        src_ref=src, dst_ref=dst, send_sem=send_sem, recv_sem=recv_sem, device_id=device, device_id_type=MESH
    )
    copy.start()
    return copy


def landed(ref, sem):
    pltpu.make_async_copy(ref, ref, sem).wait()


def inverse_factor(gram):
    n, width = gram.shape[0], 8
    row, col = (lax.broadcasted_iota(jnp.int32, (n, n), d) for d in (0, 1))
    left, right = gram, (row == col).astype(jnp.float32)
    place = lax.broadcasted_iota(jnp.int32, (width, n), 0)
    done = []
    for k in range(0, n, width):
        columns = [jnp.broadcast_to(left[:, k + j : k + j + 1], left.shape) for j in range(width)]
        heads, tails = [c[:width] for c in columns], [c[width:] for c in columns]
        left_head, right_head = left[:width], right[:width]
        left, right = left[width:], right[width:]
        pivots = jnp.zeros((width, n), jnp.float32)
        for j in range(width):
            pivot = heads[j][j : j + 1]
            over = 1.0 / pivot
            pivots = jnp.where(place == j, jnp.broadcast_to(pivot, (width, n)), pivots)
            head = jnp.where(place > j, heads[j] * over, 0.0)
            left_row, right_row = left_head[j : j + 1], right_head[j : j + 1]
            if k + width < n:
                tail = tails[j] * over
                left, right = left - tail * left_row, right - tail * right_row
            for i in range(j + 1, width):
                factor = heads[j][i : i + 1]
                heads[i] = heads[i] - head * factor
                if k + width < n:
                    tails[i] = tails[i] - tail * factor
            left_head, right_head = left_head - head * left_row, right_head - head * right_row
        done.append(right_head * lax.rsqrt(pivots))
    return jnp.concatenate(done, 0)


def normalised(slice_t, gram):
    inverse = inverse_factor(gram[...] / V)
    own = jnp.dot(inverse, slice_t[...], precision=lax.Precision.HIGHEST, preferred_element_type=f32)
    return own.T.astype(bf16)


def own_rows_in(place, own, panel):
    size = own.shape[0] // 4
    chunk = 4 * size

    def rows(core, q, m):
        start = (core * 16 + pair_index(place, q, m)) * chunk + q * size
        return panel.at[pl.ds(pl.multiple_of(start, 32), size)]

    for q in range(4):
        rows(place.c, q, 0)[...] = own[q * size : (q + 1) * size]
    return rows


def exchange_panel(place, rows, ss, rs, sc, rc):
    copies = []
    for m in (0, 1, 2, 4, 3, 5, 6, 7, 8, 9, 10, 12, 11, 13, 14, 15):
        for q in range(4):
            ref = rows(place.c, q, m)
            if m:
                landed(ref, rs.at[q, m])
            for weight, bit in ((1, 3), (2, 2), (4, 1), (8, 0)):
                if weight > m:
                    n = weight | m
                    copies.append(send(ref, ref, ss.at[q, n], rs.at[q, n], place.across(ORDERS[q][bit])))
            copies.append(send(ref, ref, sc.at[q, m], rc.at[q, m], place.sibling()))
    for q in range(4):
        for m in range(16):
            landed(rows(1 - place.c, q, m), rc.at[q, m])
    for copy in copies:
        copy.wait_send()


def panel_kernel(slice_t, gram, panel, ss, rs, sc, rc):
    place = Place()
    greeted = greet([place.sibling()] + [place.across(bit) for bit in ORDERS[0]])
    rows = own_rows_in(place, normalised(slice_t, gram), panel)
    pl.semaphore_wait(*greeted)
    exchange_panel(place, rows, ss, rs, sc, rc)


def panel_call(slice_t, gram, number):
    rank, piece = slice_t.shape
    return pl.pallas_call(
        panel_kernel,
        out_shape=jax.ShapeDtypeStruct((32 * piece, rank), bf16),
        in_specs=[VMEM, VMEM],
        out_specs=VMEM,
        scratch_shapes=[DMA((4, 16))] * 4,
        compiler_params=pltpu.CompilerParams(
            collective_id=number, has_side_effects=True, vmem_limit_bytes=VMEM_BYTES
        ),
        name=f"panel_{number}",
    )(slice_t, gram)


def sweep_kernel(first, *refs):
    lengths, block_subject, scans = refs[:3]
    if first:
        panel_in, *refs = refs[3:]
        panel = panel_in
    else:
        slice_in, gram_in, *refs = refs[3:]
        panel, sp, rp, sq, rq = refs[-5:]
        refs = refs[:-5]
    (
        z_out, g_out, held, part, got, full, away, arrived, mine, inbox, g_part, g_in, g_side, g_full,
        load_sem, s1, r1, s2, r2, sc, rc, ss, rs, sg, rg, sh, rh, si, ri,
    ) = refs
    place = Place()
    x = place.x
    rows = part.shape[1]
    owners = [lax.rem(x + step, 4) for step in (2, 1, 3, 0)]
    plane = [place.in_plane(step) for step in range(16)]
    beside = [(dx, dc, *place.along_x(dx, dc)) for dx in range(4) for dc in (0, 1) if dx or dc]
    greeted = greet([device for _, device in plane[1:]] + [device for *_, device in beside])

    def load(n):
        half = rows // 2
        at = pl.ds(pl.multiple_of(owners[n // 2] * rows + n % 2 * half, half), half)
        return pltpu.make_async_copy(scans.at[at], held.at[at], load_sem.at[n])

    ahead = 3
    for n in range(ahead if first else 8):
        load(n).start()
    if not first:
        slices = own_rows_in(place, normalised(slice_in, gram_in), panel)
        pl.semaphore_wait(*greeted)
        exchange_panel(place, slices, sp, rp, sq, rq)

    tile = 3072
    copies = []
    for t in range(4):
        for n in (2 * t, 2 * t + 1):
            if first and n + ahead < 8:
                load(n + ahead).start()
            load(n).wait()

        def add(k, acc, t=t):
            at = pl.multiple_of(k * tile, tile)
            own_rows = pl.ds(pl.multiple_of(owners[t] * rows, rows), rows)
            return acc + jnp.dot(held[own_rows, pl.ds(at, tile)], panel[pl.ds(at, tile), :], preferred_element_type=f32)

        part[t] = lax.fori_loop(0, panel.shape[0] // tile, add, jnp.zeros(part.shape[1:], f32))
        if t == 0 and first:
            pl.semaphore_wait(*greeted)
        if t < 3:
            copies.append(send(part.at[t], got.at[t], s1.at[t], r1.at[t], {"vox": owners[t]}))
    total = part[3]
    for t in range(3):
        copies[t].wait()
        total = total + got[t]
    length = lengths[block_subject[lax.axis_index("subj")]]
    time_ids = x * rows + lax.broadcasted_iota(jnp.int32, total.shape, 0)
    full[x] = jnp.where(time_ids < length, total, f32(0.0)).astype(bf16)
    copies = [send(full.at[x], full.at[x], s2.at[t], r2.at[t], {"vox": owners[t]}) for t in range(3)]
    for copy in copies:
        copy.wait()
    left = jnp.concatenate([full[i] for i in range(4)], 0).T

    rank, piece = z_out.shape
    quarter, width = rank // 4, 4 * piece
    z_flips = (("za", "zb"), ("za",), ("zb",), ())
    z_far = [place.flipped(flips)[0] for flips in z_flips]
    copies, core_copies = [], {}
    pair = [[pair_index(place, q, m) for m in range(16)] for q in range(4)]

    def pass_on(q, m):
        bit = ORDERS[q][4 - m.bit_length()]
        copies.append(send(mine.at[q, pair[q][m]], inbox.at[q, m], ss.at[q, m], rs.at[q, m], place.across(bit)))

    for away_side, k in ((1, 0), (1, 1), (0, 0), (1, 2), (0, 1), (1, 3), (0, 2), (0, 3)):
        core = 1 - place.c if away_side else place.c
        start = pl.multiple_of((core * 16 + z_far[k] * 4) * piece, width)
        block = jnp.dot(left, held[:, pl.ds(start, width)], preferred_element_type=f32)
        if not away_side:
            core_copies[k].wait()
        for y in range(4):
            for q in range(4):
                value = block[q * quarter : (q + 1) * quarter, y * piece : (y + 1) * piece]
                if away_side:
                    away[k, q, y] = value
                else:
                    mine[q, z_far[k] * 4 + y] = value + arrived[k, q, y]
        if away_side:
            core_copies[k] = send(away.at[k], arrived.at[k], sc.at[k], rc.at[k], place.sibling())
            continue
        for m in range(15, 7, -1):
            for q in range(4):
                if tuple(bit for bit in ("za", "zb") if bit in flips_of(ORDERS[q], m)) == z_flips[k]:
                    pass_on(q, m)

    for m in range(7, -1, -1):
        for q in range(4):
            value = mine[q, pair[q][m]]
            for weight in WEIGHTS:
                if weight > m:
                    landed(inbox.at[q, weight | m], rs.at[q, weight | m])
                    value = value + inbox[q, weight | m]
            if m:
                mine[q, pair[q][m]] = value
                pass_on(q, m)
            else:
                z_out[q * quarter : (q + 1) * quarter, :] = value

    own = z_out[...]
    gram = lax.dot_general(own, own, (((1,), (1,)), ((), ())), precision=lax.Precision.HIGHEST, preferred_element_type=f32)
    for p in range(16):
        g_part[p] = gram[8 * p : 8 * p + 8]
    here = plane[0][0]
    moved = [send(g_part.at[plane[r][0]], g_in.at[r], sg.at[r], rg.at[r], plane[r][1]) for r in range(1, 16)]
    for copy in copies:
        copy.wait_send()
    total = g_part[here]
    for r in range(1, 16):
        moved[r - 1].wait()
        total = total + g_in[r]
    me = x * 2 + place.c
    g_side[me] = total
    moved = [send(g_side.at[me], g_side.at[me], sh.at[n], rh.at[me], to[3]) for n, to in enumerate(beside)]
    for copy in moved:
        copy.wait_send()
    for to in beside:
        landed(g_side.at[to[2]], rh.at[to[2]])
    total = g_side[0]
    for n in range(1, 8):
        total = total + g_side[n]
    g_full[here] = total
    moved = [send(g_full.at[here], g_full.at[here], si.at[r], ri.at[r], plane[r][1]) for r in range(1, 16)]
    for copy in moved:
        copy.wait()
    for p in range(16):
        g_out[8 * p : 8 * p + 8, :] = g_full[p]


def sweep_call(lengths, block_subject, scans, panel, number):
    first = len(panel) == 1
    time_rows, cols = scans.shape
    rank = 128
    piece, quarter, rows = cols // 32, rank // 4, time_rows // 4
    scratch = [
        pltpu.VMEM((time_rows, cols), bf16),
        pltpu.VMEM((4, rows, rank), f32),
        pltpu.VMEM((3, rows, rank), f32),
        pltpu.VMEM((4, rows, rank), bf16),
        pltpu.VMEM((4, 4, 4, quarter, piece), f32),
        pltpu.VMEM((4, 4, 4, quarter, piece), f32),
        pltpu.VMEM((4, 16, quarter, piece), f32),
        pltpu.VMEM((4, 16, quarter, piece), f32),
        pltpu.VMEM((16, 8, rank), f32),
        pltpu.VMEM((16, 8, rank), f32),
        pltpu.VMEM((8, 8, rank), f32),
        pltpu.VMEM((16, 8, rank), f32),
        DMA((8,)),
        *[DMA((3,))] * 4,
        *[DMA((4,))] * 2,
        *[DMA((4, 16))] * 2,
        *[DMA((16,))] * 2,
        *[DMA((8,))] * 2,
        *[DMA((16,))] * 2,
    ]
    if not first:
        scratch += [pltpu.VMEM((cols, rank), bf16), *[DMA((4, 16))] * 4]
    return pl.pallas_call(
        functools.partial(sweep_kernel, first),
        out_shape=(jax.ShapeDtypeStruct((rank, piece), f32), jax.ShapeDtypeStruct((rank, rank), f32)),
        in_specs=[SMEM, SMEM, ANY] + [VMEM] * len(panel),
        out_specs=(VMEM, VMEM),
        scratch_shapes=scratch,
        compiler_params=pltpu.CompilerParams(
            collective_id=number, has_side_effects=True, vmem_limit_bytes=VMEM_BYTES
        ),
        name=f"sweep_{number}",
    )(lengths, block_subject, scans, *panel)


def on_device(scans, test_matrix, lengths, block_subject):
    panel = (test_matrix,)
    for sweep in range(PASSES):
        panel = sweep_call(lengths, block_subject, scans, panel, sweep)
    return panel_call(*panel, PASSES).astype(f32)


def solution(mesh):
    placed = (P("subj", "vox"), P("vox", None), P(), P())
    return jax.shard_map(
        on_device, mesh=mesh, in_specs=placed, out_specs=P("vox", None), check_vma=False
    )
```

```python
import jax
import jax.numpy as jnp
from jax import lax
from jax.experimental import pallas as pl
from jax.experimental.pallas import tpu as pltpu
from jax.sharding import PartitionSpec as P

V = 49152
PASSES = 2
MESH = pl.DeviceIdType.MESH
VMEM_BYTES = 46 * 2**20
ANY = pl.BlockSpec(memory_space=pl.ANY)
VMEM = pl.BlockSpec(memory_space=pltpu.VMEM)
SMEM = pl.BlockSpec(memory_space=pltpu.SMEM)
DMA = pltpu.SemaphoreType.DMA
f32, bf16 = jnp.float32, jnp.bfloat16
ORDERS = (("ya", "yb", "za", "zb"), ("yb", "ya", "zb", "za"), ("za", "zb", "ya", "yb"), ("zb", "za", "yb", "ya"))
WEIGHTS = (8, 4, 2, 1)


def flip_a(i):
    return i + 1 - 2 * lax.rem(i, 2)


def flip_b(i):
    return 3 - i


class Place:
    def __init__(self):
        here = lax.axis_index("subj")
        self.z, self.y, self.c = lax.div(here, 8), lax.rem(lax.div(here, 2), 4), lax.rem(here, 2)
        self.x = lax.axis_index("vox")

    def flipped(self, bits):
        z, y = self.z, self.y
        z = flip_a(z) if "za" in bits else z
        z = flip_b(z) if "zb" in bits else z
        y = flip_a(y) if "ya" in bits else y
        y = flip_b(y) if "yb" in bits else y
        return z, y

    def across(self, bit):
        z, y = self.flipped((bit,))
        return {"subj": z * 8 + y * 2 + self.c}

    def sibling(self):
        return {"subj": self.z * 8 + self.y * 2 + 1 - self.c}

    def in_plane(self, step):
        z, y = lax.rem(self.z + step // 4, 4), lax.rem(self.y + step % 4, 4)
        return z * 4 + y, {"subj": z * 8 + y * 2 + self.c}

    def along_x(self, step, other_core):
        x = lax.rem(self.x + step, 4)
        c = 1 - self.c if other_core else self.c
        return x * 2 + c, {"subj": self.z * 8 + self.y * 2 + c, "vox": x}


def flips_of(order, m):
    return tuple(bit for weight, bit in zip(WEIGHTS, order) if m & weight)


def pair_index(place, q, m):
    z, y = place.flipped(flips_of(ORDERS[q], m))
    return z * 4 + y


def greet(devices):
    barrier = pltpu.get_barrier_semaphore()
    for device in devices:
        pl.semaphore_signal(barrier, inc=1, device_id=device, device_id_type=MESH)
    return barrier, len(devices)


def send(src, dst, send_sem, recv_sem, device):
    copy = pltpu.make_async_remote_copy(
        src_ref=src, dst_ref=dst, send_sem=send_sem, recv_sem=recv_sem, device_id=device, device_id_type=MESH
    )
    copy.start()
    return copy


def landed(ref, sem):
    pltpu.make_async_copy(ref, ref, sem).wait()


def inverse_factor(gram):
    n, width = gram.shape[0], 8
    row, col = (lax.broadcasted_iota(jnp.int32, (n, n), d) for d in (0, 1))
    left, right = gram, (row == col).astype(jnp.float32)
    place = lax.broadcasted_iota(jnp.int32, (width, n), 0)
    done = []
    for k in range(0, n, width):
        columns = [jnp.broadcast_to(left[:, k + j : k + j + 1], left.shape) for j in range(width)]
        heads, tails = [c[:width] for c in columns], [c[width:] for c in columns]
        left_head, right_head = left[:width], right[:width]
        left, right = left[width:], right[width:]
        pivots = jnp.zeros((width, n), jnp.float32)
        for j in range(width):
            pivot = heads[j][j : j + 1]
            over = 1.0 / pivot
            pivots = jnp.where(place == j, jnp.broadcast_to(pivot, (width, n)), pivots)
            head = jnp.where(place > j, heads[j] * over, 0.0)
            left_row, right_row = left_head[j : j + 1], right_head[j : j + 1]
            if k + width < n:
                tail = tails[j] * over
                left, right = left - tail * left_row, right - tail * right_row
            for i in range(j + 1, width):
                factor = heads[j][i : i + 1]
                heads[i] = heads[i] - head * factor
                if k + width < n:
                    tails[i] = tails[i] - tail * factor
            left_head, right_head = left_head - head * left_row, right_head - head * right_row
        done.append(right_head * lax.rsqrt(pivots))
    return jnp.concatenate(done, 0)


def normalised(slice_t, gram):
    inverse = inverse_factor(gram / V)
    own = jnp.dot(inverse, slice_t[...], precision=lax.Precision.HIGHEST, preferred_element_type=f32)
    return own.T.astype(bf16)


def own_rows_in(place, own, panel):
    size = own.shape[0] // 4
    chunk = 4 * size

    def rows(core, q, m):
        start = (core * 16 + pair_index(place, q, m)) * chunk + q * size
        return panel.at[pl.ds(pl.multiple_of(start, 32), size)]

    for q in range(4):
        rows(place.c, q, 0)[...] = own[q * size : (q + 1) * size]
    return rows


def exchange_panel(place, rows, ss, rs, sc, rc):
    copies = []
    for m in (0, 1, 2, 4, 3, 5, 6, 7, 8, 9, 10, 12, 11, 13, 14, 15):
        for q in range(4):
            ref = rows(place.c, q, m)
            if m:
                landed(ref, rs.at[q, m])
            for weight, bit in ((1, 3), (2, 2), (4, 1), (8, 0)):
                if weight > m:
                    n = weight | m
                    copies.append(send(ref, ref, ss.at[q, n], rs.at[q, n], place.across(ORDERS[q][bit])))
            copies.append(send(ref, ref, sc.at[q, m], rc.at[q, m], place.sibling()))
    for q in range(4):
        for m in range(16):
            landed(rows(1 - place.c, q, m), rc.at[q, m])
    for copy in copies:
        copy.wait_send()


def whole_kernel(lengths, block_subject, scans, first_panel, out, *scratch):
    (
        held, panel, own_t, part, got, full, away, arrived, mine, inbox, g_part, g_in, g_side, g_full,
        load_sem, s1, r1, s2, r2, sc, rc, ss, rs, sg, rg, sh, rh, si, ri, sp, rp, sq, rq,
    ) = scratch
    place = Place()
    x = place.x
    rows = part.shape[1]
    rank, piece = own_t.shape
    quarter, width = rank // 4, 4 * piece
    owners = [lax.rem(x + step, 4) for step in (2, 1, 3, 0)]
    plane = [place.in_plane(step) for step in range(16)]
    beside = [(dx, dc, *place.along_x(dx, dc)) for dx in range(4) for dc in (0, 1) if dx or dc]
    greeted = greet([device for _, device in plane[1:]] + [device for *_, device in beside])

    def load(n):
        half = rows // 2
        at = pl.ds(pl.multiple_of(owners[n // 2] * rows + n % 2 * half, half), half)
        return pltpu.make_async_copy(scans.at[at], held.at[at], load_sem.at[n])

    ahead = 3
    for n in range(ahead):
        load(n).start()
    for sweep in range(PASSES):
        source = first_panel if sweep == 0 else panel
        tile = 3072
        copies = []
        for t in range(4):
            for n in (2 * t, 2 * t + 1):
                if sweep == 0 and n + ahead < 8:
                    load(n + ahead).start()
                if sweep == 0:
                    load(n).wait()

            def add(k, acc, t=t, source=source):
                at = pl.multiple_of(k * tile, tile)
                own_rows = pl.ds(pl.multiple_of(owners[t] * rows, rows), rows)
                return acc + jnp.dot(held[own_rows, pl.ds(at, tile)], source[pl.ds(at, tile), :], preferred_element_type=f32)

            part[t] = lax.fori_loop(0, source.shape[0] // tile, add, jnp.zeros(part.shape[1:], f32))
            if t == 0 and sweep == 0:
                pl.semaphore_wait(*greeted)
            if t < 3:
                copies.append(send(part.at[t], got.at[t], s1.at[t], r1.at[t], {"vox": owners[t]}))
        total = part[3]
        for t in range(3):
            copies[t].wait()
            total = total + got[t]
        length = lengths[block_subject[lax.axis_index("subj")]]
        time_ids = x * rows + lax.broadcasted_iota(jnp.int32, total.shape, 0)
        full[x] = jnp.where(time_ids < length, total, f32(0.0)).astype(bf16)
        copies = [send(full.at[x], full.at[x], s2.at[t], r2.at[t], {"vox": owners[t]}) for t in range(3)]
        for copy in copies:
            copy.wait()
        left = jnp.concatenate([full[i] for i in range(4)], 0).T

        z_flips = (("za", "zb"), ("za",), ("zb",), ())
        z_far = [place.flipped(flips)[0] for flips in z_flips]
        copies, core_copies = [], {}
        pair = [[pair_index(place, q, m) for m in range(16)] for q in range(4)]

        def pass_on(q, m, copies=copies):
            bit = ORDERS[q][4 - m.bit_length()]
            copies.append(send(mine.at[q, pair[q][m]], inbox.at[q, m], ss.at[q, m], rs.at[q, m], place.across(bit)))

        for away_side, k in ((1, 0), (1, 1), (0, 0), (1, 2), (0, 1), (1, 3), (0, 2), (0, 3)):
            core = 1 - place.c if away_side else place.c
            start = pl.multiple_of((core * 16 + z_far[k] * 4) * piece, width)
            block = jnp.dot(left, held[:, pl.ds(start, width)], preferred_element_type=f32)
            if not away_side:
                core_copies[k].wait()
            for y in range(4):
                for q in range(4):
                    value = block[q * quarter : (q + 1) * quarter, y * piece : (y + 1) * piece]
                    if away_side:
                        away[k, q, y] = value
                    else:
                        mine[q, z_far[k] * 4 + y] = value + arrived[k, q, y]
            if away_side:
                core_copies[k] = send(away.at[k], arrived.at[k], sc.at[k], rc.at[k], place.sibling())
                continue
            for m in range(15, 7, -1):
                for q in range(4):
                    if tuple(bit for bit in ("za", "zb") if bit in flips_of(ORDERS[q], m)) == z_flips[k]:
                        pass_on(q, m)

        for m in range(7, -1, -1):
            for q in range(4):
                value = mine[q, pair[q][m]]
                for weight in WEIGHTS:
                    if weight > m:
                        landed(inbox.at[q, weight | m], rs.at[q, weight | m])
                        value = value + inbox[q, weight | m]
                if m:
                    mine[q, pair[q][m]] = value
                    pass_on(q, m)
                else:
                    own_t[q * quarter : (q + 1) * quarter, :] = value

        own = own_t[...]
        gram = lax.dot_general(own, own, (((1,), (1,)), ((), ())), precision=lax.Precision.HIGHEST, preferred_element_type=f32)
        for p in range(16):
            g_part[p] = gram[8 * p : 8 * p + 8]
        here = plane[0][0]
        moved = [send(g_part.at[plane[r][0]], g_in.at[r], sg.at[r], rg.at[r], plane[r][1]) for r in range(1, 16)]
        for copy in copies:
            copy.wait_send()
        total = g_part[here]
        for r in range(1, 16):
            moved[r - 1].wait()
            total = total + g_in[r]
        me = x * 2 + place.c
        g_side[me] = total
        moved = [send(g_side.at[me], g_side.at[me], sh.at[n], rh.at[me], to[3]) for n, to in enumerate(beside)]
        for copy in moved:
            copy.wait_send()
        for to in beside:
            landed(g_side.at[to[2]], rh.at[to[2]])
        total = g_side[0]
        for n in range(1, 8):
            total = total + g_side[n]
        g_full[here] = total
        moved = [send(g_full.at[here], g_full.at[here], si.at[r], ri.at[r], plane[r][1]) for r in range(1, 16)]
        for copy in moved:
            copy.wait()

        target = out if sweep == PASSES - 1 else panel
        gram = jnp.concatenate([g_full[p] for p in range(16)], 0)
        slices = own_rows_in(place, normalised(own_t, gram), target)
        exchange_panel(place, slices, sp, rp, sq, rq)


def whole_call(lengths, block_subject, scans, panel):
    time_rows, cols = scans.shape
    rank = panel.shape[1]
    piece, quarter, rows = cols // 32, rank // 4, time_rows // 4
    return pl.pallas_call(
        whole_kernel,
        out_shape=jax.ShapeDtypeStruct((cols, rank), bf16),
        in_specs=[SMEM, SMEM, ANY, VMEM],
        out_specs=VMEM,
        scratch_shapes=[
            pltpu.VMEM((time_rows, cols), bf16),
            pltpu.VMEM((cols, rank), bf16),
            pltpu.VMEM((rank, piece), f32),
            pltpu.VMEM((4, rows, rank), f32),
            pltpu.VMEM((3, rows, rank), f32),
            pltpu.VMEM((4, rows, rank), bf16),
            pltpu.VMEM((4, 4, 4, quarter, piece), f32),
            pltpu.VMEM((4, 4, 4, quarter, piece), f32),
            pltpu.VMEM((4, 16, quarter, piece), f32),
            pltpu.VMEM((4, 16, quarter, piece), f32),
            pltpu.VMEM((16, 8, rank), f32),
            pltpu.VMEM((16, 8, rank), f32),
            pltpu.VMEM((8, 8, rank), f32),
            pltpu.VMEM((16, 8, rank), f32),
            DMA((8,)),
            *[DMA((3,))] * 4,
            *[DMA((4,))] * 2,
            *[DMA((4, 16))] * 2,
            *[DMA((16,))] * 2,
            *[DMA((8,))] * 2,
            *[DMA((16,))] * 2,
            *[DMA((4, 16))] * 4,
        ],
        compiler_params=pltpu.CompilerParams(
            collective_id=0, has_side_effects=True, vmem_limit_bytes=VMEM_BYTES
        ),
        name="range_finder",
    )(lengths, block_subject, scans, panel)


def on_device(scans, test_matrix, lengths, block_subject):
    return whole_call(lengths, block_subject, scans, test_matrix).astype(f32)


def solution(mesh):
    placed = (P("subj", "vox"), P("vox", None), P(), P())
    return jax.shard_map(
        on_device, mesh=mesh, in_specs=placed, out_specs=P("vox", None), check_vma=False
    )
```

```python
import jax
import jax.numpy as jnp
from jax import lax
from jax.experimental import pallas as pl
from jax.experimental.pallas import tpu as pltpu
from jax.sharding import PartitionSpec as P

V = 49152
PASSES = 2
MESH = pl.DeviceIdType.MESH
VMEM_BYTES = 46 * 2**20
VMEM = pl.BlockSpec(memory_space=pltpu.VMEM)
HBM = pl.BlockSpec(memory_space=pltpu.HBM)
DMA = pltpu.SemaphoreType.DMA
f32, bf16 = jnp.float32, jnp.bfloat16
ORDERS = (("ya", "yb", "za", "zb"), ("yb", "ya", "zb", "za"), ("za", "zb", "ya", "yb"), ("zb", "za", "yb", "ya"))
WEIGHTS = (8, 4, 2, 1)


def flip_a(i):
    return i + 1 - 2 * lax.rem(i, 2)


def flip_b(i):
    return 3 - i


class Place:
    def __init__(self):
        here = lax.axis_index("subj")
        self.z, self.y, self.c = lax.div(here, 8), lax.rem(lax.div(here, 2), 4), lax.rem(here, 2)
        self.x = lax.axis_index("vox")

    def flipped(self, bits):
        z, y = self.z, self.y
        z = flip_a(z) if "za" in bits else z
        z = flip_b(z) if "zb" in bits else z
        y = flip_a(y) if "ya" in bits else y
        y = flip_b(y) if "yb" in bits else y
        return z, y

    def across(self, bit):
        z, y = self.flipped((bit,))
        return {"subj": z * 8 + y * 2 + self.c}

    def sibling(self):
        return {"subj": self.z * 8 + self.y * 2 + 1 - self.c}

    def in_plane(self, step):
        z, y = lax.rem(self.z + step // 4, 4), lax.rem(self.y + step % 4, 4)
        return z * 4 + y, {"subj": z * 8 + y * 2 + self.c}

    def along_x(self, step, other_core):
        x = lax.rem(self.x + step, 4)
        c = 1 - self.c if other_core else self.c
        return x * 2 + c, {"subj": self.z * 8 + self.y * 2 + c, "vox": x}


def flips_of(order, m):
    return tuple(bit for weight, bit in zip(WEIGHTS, order) if m & weight)


def pair_index(place, q, m):
    z, y = place.flipped(flips_of(ORDERS[q], m))
    return z * 4 + y


def greet(devices):
    barrier = pltpu.get_barrier_semaphore()
    for device in devices:
        pl.semaphore_signal(barrier, inc=1, device_id=device, device_id_type=MESH)
    return barrier, len(devices)


def send(src, dst, send_sem, recv_sem, device):
    copy = pltpu.make_async_remote_copy(
        src_ref=src, dst_ref=dst, send_sem=send_sem, recv_sem=recv_sem, device_id=device, device_id_type=MESH
    )
    copy.start()
    return copy


def landed(ref, sem):
    pltpu.make_async_copy(ref, ref, sem).wait()


def inverse_factor(gram):
    n, width = gram.shape[0], 8
    row, col = (lax.broadcasted_iota(jnp.int32, (n, n), d) for d in (0, 1))
    left, right = gram, (row == col).astype(jnp.float32)
    place = lax.broadcasted_iota(jnp.int32, (width, n), 0)
    done = []
    for k in range(0, n, width):
        columns = [jnp.broadcast_to(left[:, k + j : k + j + 1], left.shape) for j in range(width)]
        heads, tails = [c[:width] for c in columns], [c[width:] for c in columns]
        left_head, right_head = left[:width], right[:width]
        left, right = left[width:], right[width:]
        pivots = jnp.zeros((width, n), jnp.float32)
        for j in range(width):
            pivot = heads[j][j : j + 1]
            over = 1.0 / pivot
            pivots = jnp.where(place == j, jnp.broadcast_to(pivot, (width, n)), pivots)
            head = jnp.where(place > j, heads[j] * over, 0.0)
            left_row, right_row = left_head[j : j + 1], right_head[j : j + 1]
            if k + width < n:
                tail = tails[j] * over
                left, right = left - tail * left_row, right - tail * right_row
            for i in range(j + 1, width):
                factor = heads[j][i : i + 1]
                heads[i] = heads[i] - head * factor
                if k + width < n:
                    tails[i] = tails[i] - tail * factor
            left_head, right_head = left_head - head * left_row, right_head - head * right_row
        done.append(right_head * lax.rsqrt(pivots))
    return jnp.concatenate(done, 0)


def normalised(slice_t, gram):
    inverse = inverse_factor(gram / V)
    own = jnp.dot(inverse, slice_t[...], precision=lax.Precision.HIGHEST, preferred_element_type=f32)
    return own.T.astype(bf16)


def own_rows_in(place, own, panel):
    size = own.shape[0] // 4
    chunk = 4 * size

    def rows(core, q, m):
        start = (core * 16 + pair_index(place, q, m)) * chunk + q * size
        return panel.at[pl.ds(pl.multiple_of(start, 32), size)]

    for q in range(4):
        rows(place.c, q, 0)[...] = own[q * size : (q + 1) * size]
    return rows


def exchange_panel(place, rows, ss, rs, sc, rc):
    copies = []
    for m in (0, 1, 2, 4, 3, 5, 6, 7, 8, 9, 10, 12, 11, 13, 14, 15):
        for q in range(4):
            ref = rows(place.c, q, m)
            if m:
                landed(ref, rs.at[q, m])
            for weight, bit in ((1, 3), (2, 2), (4, 1), (8, 0)):
                if weight > m:
                    n = weight | m
                    copies.append(send(ref, ref, ss.at[q, n], rs.at[q, n], place.across(ORDERS[q][bit])))
            copies.append(send(ref, ref, sc.at[q, m], rc.at[q, m], place.sibling()))
    for q in range(4):
        for m in range(16):
            landed(rows(1 - place.c, q, m), rc.at[q, m])
    for copy in copies:
        copy.wait_send()


def whole_kernel(lengths_in, block_subject_in, scans, panel_in, out, *scratch):
    (
        lengths, block_subject, small_sem, first_panel, held, panel, own_t, part, got, full, away, arrived, mine, inbox, g_part, g_in, g_side, g_full,
        load_sem, s1, r1, s2, r2, sc, rc, ss, rs, sg, rg, sh, rh, si, ri, sp, rp, sq, rq,
    ) = scratch
    place = Place()
    x = place.x
    rows = part.shape[1]
    rank, piece = own_t.shape
    quarter, width = rank // 4, 4 * piece
    owners = [lax.rem(x + step, 4) for step in (2, 1, 3, 0)]
    plane = [place.in_plane(step) for step in range(16)]
    beside = [(dx, dc, *place.along_x(dx, dc)) for dx in range(4) for dc in (0, 1) if dx or dc]
    greeted = greet([device for _, device in plane[1:]] + [device for *_, device in beside])

    def load(n):
        half = rows // 2
        at = pl.ds(pl.multiple_of(owners[n // 2] * rows + n % 2 * half, half), half)
        return pltpu.make_async_copy(scans.at[at], held.at[at], load_sem.at[n])

    small = [
        pltpu.make_async_copy(panel_in, first_panel, small_sem.at[0]),
        pltpu.make_async_copy(lengths_in, lengths, small_sem.at[1]),
        pltpu.make_async_copy(block_subject_in, block_subject, small_sem.at[2]),
    ]
    for copy in small:
        copy.start()
    ahead = 3
    for n in range(ahead):
        load(n).start()
    for copy in small:
        copy.wait()
    for sweep in range(PASSES):
        source = first_panel if sweep == 0 else panel
        copies = []
        for t in range(4):
            for n in (2 * t, 2 * t + 1):
                if sweep == 0 and n + ahead < 8:
                    load(n + ahead).start()
                if sweep == 0:
                    load(n).wait()

            own_rows = pl.ds(pl.multiple_of(owners[t] * rows, rows), rows)
            tile = source.shape[0] // 2

            def add(k, acc, own_rows=own_rows, source=source, tile=tile):
                at = pl.ds(pl.multiple_of(k * tile, tile), tile)
                return acc + jnp.dot(held[own_rows, at], source[at, :], preferred_element_type=f32)

            part[t] = lax.fori_loop(0, 2, add, jnp.zeros(part.shape[1:], f32))
            if t == 0 and sweep == 0:
                pl.semaphore_wait(*greeted)
            if t < 3:
                copies.append(send(part.at[t], got.at[t], s1.at[t], r1.at[t], {"vox": owners[t]}))
        total = part[3]
        for t in range(3):
            copies[t].wait()
            total = total + got[t]
        length = lengths[block_subject[lax.axis_index("subj")]]
        time_ids = x * rows + lax.broadcasted_iota(jnp.int32, total.shape, 0)
        full[x] = jnp.where(time_ids < length, total, f32(0.0)).astype(bf16)
        copies = [send(full.at[x], full.at[x], s2.at[t], r2.at[t], {"vox": owners[t]}) for t in range(3)]
        for copy in copies:
            copy.wait()
        left = jnp.concatenate([full[i] for i in range(4)], 0).T

        z_flips = (("za", "zb"), ("za",), ("zb",), ())
        z_far = [place.flipped(flips)[0] for flips in z_flips]
        copies, core_copies = [], {}
        pair = [[pair_index(place, q, m) for m in range(16)] for q in range(4)]

        def pass_on(q, m, copies=copies):
            bit = ORDERS[q][4 - m.bit_length()]
            copies.append(send(mine.at[q, pair[q][m]], inbox.at[q, m], ss.at[q, m], rs.at[q, m], place.across(bit)))

        for away_side, k in ((1, 0), (1, 1), (0, 0), (1, 2), (0, 1), (1, 3), (0, 2), (0, 3)):
            core = 1 - place.c if away_side else place.c
            start = pl.multiple_of((core * 16 + z_far[k] * 4) * piece, width)
            block = jnp.dot(left, held[:, pl.ds(start, width)], preferred_element_type=f32)
            if not away_side:
                core_copies[k].wait()
            for y in range(4):
                for q in range(4):
                    value = block[q * quarter : (q + 1) * quarter, y * piece : (y + 1) * piece]
                    if away_side:
                        away[k, q, y] = value
                    else:
                        mine[q, z_far[k] * 4 + y] = value + arrived[k, q, y]
            if away_side:
                core_copies[k] = send(away.at[k], arrived.at[k], sc.at[k], rc.at[k], place.sibling())
                continue
            for m in range(15, 11, -1):
                for q in range(4):
                    if tuple(bit for bit in ("za", "zb") if bit in flips_of(ORDERS[q], m)) == z_flips[k]:
                        pass_on(q, m)

        for m in (7, 6, 5, 3, 4, 2, 1, 0):
            for q in range(4):
                value = mine[q, pair[q][m]]
                for weight in WEIGHTS:
                    if weight > m:
                        landed(inbox.at[q, weight | m], rs.at[q, weight | m])
                        value = value + inbox[q, weight | m]
                if m:
                    mine[q, pair[q][m]] = value
                    pass_on(q, m)
                    if m > 3:
                        pass_on(q, m + 4)
                else:
                    own_t[q * quarter : (q + 1) * quarter, :] = value

        own = own_t[...]
        gram = lax.dot_general(own, own, (((1,), (1,)), ((), ())), precision=lax.Precision.HIGHEST, preferred_element_type=f32)
        for p in range(16):
            g_part[p] = gram[8 * p : 8 * p + 8]
        here = plane[0][0]
        moved = [send(g_part.at[plane[r][0]], g_in.at[r], sg.at[r], rg.at[r], plane[r][1]) for r in range(1, 16)]
        for copy in copies:
            copy.wait_send()
        total = g_part[here]
        for r in range(1, 16):
            moved[r - 1].wait()
            total = total + g_in[r]
        me = x * 2 + place.c
        g_side[me] = total
        moved = [send(g_side.at[me], g_side.at[me], sh.at[n], rh.at[me], to[3]) for n, to in enumerate(beside)]
        for copy in moved:
            copy.wait_send()
        for to in beside:
            landed(g_side.at[to[2]], rh.at[to[2]])
        total = g_side[0]
        for n in range(1, 8):
            total = total + g_side[n]
        g_full[here] = total
        moved = [send(g_full.at[here], g_full.at[here], si.at[r], ri.at[r], plane[r][1]) for r in range(1, 16)]
        for copy in moved:
            copy.wait()

        target = out if sweep == PASSES - 1 else panel
        gram = jnp.concatenate([g_full[p] for p in range(16)], 0)
        slices = own_rows_in(place, normalised(own_t, gram), target)
        exchange_panel(place, slices, sp, rp, sq, rq)


def whole_call(lengths, block_subject, scans, panel):
    time_rows, cols = scans.shape
    rank = panel.shape[1]
    piece, quarter, rows = cols // 32, rank // 4, time_rows // 4
    return pl.pallas_call(
        whole_kernel,
        out_shape=jax.ShapeDtypeStruct((cols, rank), bf16),
        in_specs=[HBM, HBM, HBM, HBM],
        out_specs=VMEM,
        scratch_shapes=[
            pltpu.SMEM(lengths.shape, jnp.int32),
            pltpu.SMEM(block_subject.shape, jnp.int32),
            DMA((3,)),
            pltpu.VMEM((cols, rank), bf16),
            pltpu.VMEM((time_rows, cols), bf16),
            pltpu.VMEM((cols, rank), bf16),
            pltpu.VMEM((rank, piece), f32),
            pltpu.VMEM((4, rows, rank), f32),
            pltpu.VMEM((3, rows, rank), f32),
            pltpu.VMEM((4, rows, rank), bf16),
            pltpu.VMEM((4, 4, 4, quarter, piece), f32),
            pltpu.VMEM((4, 4, 4, quarter, piece), f32),
            pltpu.VMEM((4, 16, quarter, piece), f32),
            pltpu.VMEM((4, 16, quarter, piece), f32),
            pltpu.VMEM((16, 8, rank), f32),
            pltpu.VMEM((16, 8, rank), f32),
            pltpu.VMEM((8, 8, rank), f32),
            pltpu.VMEM((16, 8, rank), f32),
            DMA((8,)),
            *[DMA((3,))] * 4,
            *[DMA((4,))] * 2,
            *[DMA((4, 16))] * 2,
            *[DMA((16,))] * 2,
            *[DMA((8,))] * 2,
            *[DMA((16,))] * 2,
            *[DMA((4, 16))] * 4,
        ],
        compiler_params=pltpu.CompilerParams(
            collective_id=0, has_side_effects=True, vmem_limit_bytes=VMEM_BYTES
        ),
        name="range_finder",
    )(lengths, block_subject, scans, panel)


def on_device(scans, test_matrix, lengths, block_subject):
    lengths, block_subject, test_matrix = (
        pltpu.with_memory_space_constraint(a, pltpu.HBM) for a in (lengths, block_subject, test_matrix)
    )
    return whole_call(lengths, block_subject, scans, test_matrix).astype(f32)


def solution(mesh):
    placed = (P("subj", "vox"), P("vox", None), P(), P())
    return jax.shard_map(
        on_device, mesh=mesh, in_specs=placed, out_specs=P("vox", None), check_vma=False
    )
```

```python
import jax
import jax.numpy as jnp
from jax import lax
from jax.experimental import pallas as pl
from jax.experimental.pallas import tpu as pltpu
from jax.sharding import PartitionSpec as P

V = 49152
PASSES = 2
MESH = pl.DeviceIdType.MESH
VMEM_BYTES = 46 * 2**20
VMEM = pl.BlockSpec(memory_space=pltpu.VMEM)
HBM = pl.BlockSpec(memory_space=pltpu.HBM)
DMA = pltpu.SemaphoreType.DMA
f32, bf16 = jnp.float32, jnp.bfloat16
ORDERS = (("ya", "yb", "za", "zb"), ("yb", "ya", "zb", "za"), ("za", "zb", "ya", "yb"), ("zb", "za", "yb", "ya"))
WEIGHTS = (8, 4, 2, 1)


def flip_a(i):
    return i + 1 - 2 * lax.rem(i, 2)


def flip_b(i):
    return 3 - i


class Place:
    def __init__(self):
        here = lax.axis_index("subj")
        self.z, self.y, self.c = lax.div(here, 8), lax.rem(lax.div(here, 2), 4), lax.rem(here, 2)
        self.x = lax.axis_index("vox")

        self.zs = {(): self.z, ("za",): flip_a(self.z), ("zb",): flip_b(self.z)}
        self.zs["za", "zb"] = flip_b(self.zs[("za",)])
        self.ys = {(): self.y, ("ya",): flip_a(self.y), ("yb",): flip_b(self.y)}
        self.ys["ya", "yb"] = flip_b(self.ys[("ya",)])
        self.to = {
            bit: {"subj": (self.zs if bit[0] == "z" else self.ys)[(bit,)] * (8 if bit[0] == "z" else 2) + rest + self.c}
            for bit in ORDERS[0]
            for rest in [self.y * 2 if bit[0] == "z" else self.z * 8]
        }
        self.pairs = {
            zf + yf: z * 4 + y for zf, z in self.zs.items() for yf, y in self.ys.items()
        }
        self.beside_core = {"subj": here + 1 - 2 * self.c}

    def across(self, bit):
        return self.to[bit]

    def sibling(self):
        return self.beside_core

    def in_plane(self, step):
        z, y = lax.rem(self.z + step // 4, 4), lax.rem(self.y + step % 4, 4)
        return z * 4 + y, {"subj": z * 8 + y * 2 + self.c}

    def along_x(self, step, other_core):
        x = lax.rem(self.x + step, 4)
        c = 1 - self.c if other_core else self.c
        return x * 2 + c, {"subj": self.z * 8 + self.y * 2 + c, "vox": x}


def flips_of(order, m):
    flips = [bit for weight, bit in zip(WEIGHTS, order) if m & weight]
    return tuple(bit for bit in ("za", "zb", "ya", "yb") if bit in flips)


def pair_index(place, q, m):
    return place.pairs[flips_of(ORDERS[q], m)]


def greet(devices):
    barrier = pltpu.get_barrier_semaphore()
    for device in devices:
        pl.semaphore_signal(barrier, inc=1, device_id=device, device_id_type=MESH)
    return barrier, len(devices)


def send(src, dst, send_sem, recv_sem, device):
    copy = pltpu.make_async_remote_copy(
        src_ref=src, dst_ref=dst, send_sem=send_sem, recv_sem=recv_sem, device_id=device, device_id_type=MESH
    )
    copy.start()
    return copy


def landed(ref, sem):
    pltpu.make_async_copy(ref, ref, sem).wait()


def inverse_factor(gram):
    n, width = gram.shape[0], 8
    row, col = (lax.broadcasted_iota(jnp.int32, (n, n), d) for d in (0, 1))
    left, right = gram, (row == col).astype(jnp.float32)
    place = lax.broadcasted_iota(jnp.int32, (width, n), 0)
    done = []
    for k in range(0, n, width):
        columns = [jnp.broadcast_to(left[:, k + j : k + j + 1], left.shape) for j in range(width)]
        heads, tails = [c[:width] for c in columns], [c[width:] for c in columns]
        left_head, right_head = left[:width], right[:width]
        left, right = left[width:], right[width:]
        pivots = jnp.zeros((width, n), jnp.float32)
        for j in range(width):
            pivot = heads[j][j : j + 1]
            over = 1.0 / pivot
            pivots = jnp.where(place == j, jnp.broadcast_to(pivot, (width, n)), pivots)
            head = jnp.where(place > j, heads[j] * over, 0.0)
            left_row, right_row = left_head[j : j + 1], right_head[j : j + 1]
            if k + width < n:
                tail = tails[j] * over
                left, right = left - tail * left_row, right - tail * right_row
            for i in range(j + 1, width):
                factor = heads[j][i : i + 1]
                heads[i] = heads[i] - head * factor
                if k + width < n:
                    tails[i] = tails[i] - tail * factor
            left_head, right_head = left_head - head * left_row, right_head - head * right_row
        done.append(right_head * lax.rsqrt(pivots))
    return jnp.concatenate(done, 0)


def normalised(slice_t, gram):
    inverse = inverse_factor(gram / V)
    own = jnp.dot(inverse, slice_t[...], precision=lax.Precision.HIGHEST, preferred_element_type=f32)
    return own.T.astype(bf16)


def exchange_panel(place, own, panel, ss, rs, sc, rc):
    chunk = own.shape[0]
    size = chunk // 4

    def rows(core, pair, q=None):
        start = (core * 16 + pair) * chunk
        if q is None:
            return panel.at[pl.ds(pl.multiple_of(start, 32), chunk)]
        return panel.at[pl.ds(pl.multiple_of(start + q * size, 32), size)]

    def pass_on(q, m, weight):
        ref = rows(place.c, pair_index(place, q, m), q)
        device = {"subj": place.pairs[flips_of(ORDERS[q], weight)] * 2 + place.c}
        send(ref, ref, ss.at[q], rs.at[q, weight | m], device)

    rows(place.c, place.pairs[()])[...] = own
    for weight in (1, 2, 3, 4, 8):
        for q in range(4):
            pass_on(q, 0, weight)
    for m in range(16):
        for q in range(4):
            if m:
                landed(rows(place.c, pair_index(place, q, m), q), rs.at[q, m])
                for weight in (4, 8):
                    if weight > m:
                        pass_on(q, m, weight)
        for flips, pair in place.pairs.items():
            if m == max(sum(w for w, bit in zip(WEIGHTS, order) if bit in flips) for order in ORDERS):
                send(rows(place.c, pair), rows(place.c, pair), sc.at[0], rc.at[0], place.sibling())
    half = panel.at[pl.ds(0, 16 * chunk)]
    for q in range(4):
        landed(panel.at[pl.ds(0, 15 * size)], ss.at[q])
    landed(half, sc.at[0])
    landed(half, rc.at[0])


def whole_kernel(lengths_in, block_subject_in, scans, panel_in, out, *scratch):
    (
        lengths, block_subject, small_sem, first_panel, held, panel, own_t, part, got, full, away, arrived, mine, inbox, g_part, g_in, g_plane, g_full,
        load_sem, s1, r1, s2, r2, sc, rc, ss, rs, sg, rg, sh, rh, si, ri, sp, rp, sq, rq,
    ) = scratch
    place = Place()
    x = place.x
    rows = part.shape[1]
    rank, piece = own_t.shape
    quarter, width = rank // 4, 4 * piece
    owners = [lax.rem(x + step, 4) for step in (2, 1, 3, 0)]
    plane = [place.in_plane(step) for step in range(16)]
    beside = [(dx, dc, *place.along_x(dx, dc)) for dx in range(4) for dc in (0, 1) if dx or dc]
    greeted = greet([device for _, device in plane[1:]] + [device for *_, device in beside])

    def load(n):
        half = rows // 2
        at = pl.ds(pl.multiple_of(owners[n // 2] * rows + n % 2 * half, half), half)
        return pltpu.make_async_copy(scans.at[at], held.at[at], load_sem.at[n])

    small = [
        pltpu.make_async_copy(panel_in, first_panel, small_sem.at[0]),
        pltpu.make_async_copy(lengths_in, lengths, small_sem.at[1]),
        pltpu.make_async_copy(block_subject_in, block_subject, small_sem.at[2]),
    ]
    for copy in small:
        copy.start()
    ahead = 3
    for n in range(ahead):
        load(n).start()
    for copy in small:
        copy.wait()
    for sweep in range(PASSES):
        source = first_panel if sweep == 0 else panel
        copies = []
        for t in range(4):
            for n in (2 * t, 2 * t + 1):
                if sweep == 0 and n + ahead < 8:
                    load(n + ahead).start()
                if sweep == 0:
                    load(n).wait()

            own_rows = pl.ds(pl.multiple_of(owners[t] * rows, rows), rows)
            tile = source.shape[0] // 2

            def add(k, acc, own_rows=own_rows, source=source, tile=tile):
                at = pl.ds(pl.multiple_of(k * tile, tile), tile)
                return acc + jnp.dot(held[own_rows, at], source[at, :], preferred_element_type=f32)

            part[t] = lax.fori_loop(0, 2, add, jnp.zeros(part.shape[1:], f32))
            if t == 0 and sweep == 0:
                pl.semaphore_wait(*greeted)
            if t < 3:
                copies.append(send(part.at[t], got.at[t], s1.at[t], r1.at[t], {"vox": owners[t]}))
        total = part[3]
        for t in range(3):
            copies[t].wait()
            total = total + got[t]
        length = lengths[block_subject[lax.axis_index("subj")]]
        time_ids = x * rows + lax.broadcasted_iota(jnp.int32, total.shape, 0)
        full[x] = jnp.where(time_ids < length, total, f32(0.0)).astype(bf16)
        copies = [send(full.at[x], full.at[x], s2.at[t], r2.at[t], {"vox": owners[t]}) for t in range(3)]
        for copy in copies:
            copy.wait()
        left = jnp.concatenate([full[i] for i in range(4)], 0).T

        z_flips = (("za", "zb"), ("za",), ("zb",), ())
        z_far = [place.zs[flips] for flips in z_flips]
        core_copies = {}
        pair = [[pair_index(place, q, m) for m in range(16)] for q in range(4)]

        def pass_on(q, m):
            bit = ORDERS[q][4 - m.bit_length()]
            send(mine.at[q, pair[q][m]], inbox.at[q, m], ss.at[q], rs.at[q, m], place.across(bit))

        for away_side, k in ((1, 0), (1, 1), (0, 0), (1, 2), (0, 1), (1, 3), (0, 2), (0, 3)):
            core = 1 - place.c if away_side else place.c
            start = pl.multiple_of((core * 16 + z_far[k] * 4) * piece, width)
            block = jnp.dot(left, held[:, pl.ds(start, width)], preferred_element_type=f32)
            if not away_side:
                core_copies[k].wait()
            for y in range(4):
                for q in range(4):
                    value = block[q * quarter : (q + 1) * quarter, y * piece : (y + 1) * piece]
                    if away_side:
                        away[k, q, y] = value
                    else:
                        mine[q, z_far[k] * 4 + y] = value + arrived[k, q, y]
            if away_side:
                core_copies[k] = send(away.at[k], arrived.at[k], sc.at[k], rc.at[k], place.sibling())
                continue
            for m in range(15, 11, -1):
                for q in range(4):
                    if tuple(bit for bit in ("za", "zb") if bit in flips_of(ORDERS[q], m)) == z_flips[k]:
                        pass_on(q, m)

        for m in (7, 6, 5, 3, 4, 2, 1, 0):
            for q in range(4):
                value = mine[q, pair[q][m]]
                for weight in WEIGHTS:
                    if weight > m:
                        landed(inbox.at[q, weight | m], rs.at[q, weight | m])
                        value = value + inbox[q, weight | m]
                if m:
                    mine[q, pair[q][m]] = value
                    pass_on(q, m)
                    if m > 3:
                        pass_on(q, m + 4)
                else:
                    own_t[q * quarter : (q + 1) * quarter, :] = value

        own = own_t[...]
        gram = lax.dot_general(own, own, (((1,), (1,)), ((), ())), precision=lax.Precision.HIGHEST, preferred_element_type=f32)
        block = rank // 8
        for p in range(8):
            g_part[p] = gram[block * p : block * (p + 1)]
        me, here = x * 2 + place.c, plane[0][0]
        moved = [send(g_part.at[to[2]], g_in.at[n], sg.at[n], rg.at[n], to[3]) for n, to in enumerate(beside)]
        for q in range(4):
            landed(mine.at[q, pl.ds(0, 15)], ss.at[q])
        total = g_part[me]
        for n, copy in enumerate(moved):
            copy.wait()
            total = total + g_in[n]
        g_plane[here] = total
        moved = [send(g_plane.at[here], g_plane.at[here], sh.at[r], rh.at[r], plane[r][1]) for r in range(1, 16)]
        for copy in moved:
            copy.wait()
        total = g_plane[0]
        for p in range(1, 16):
            total = total + g_plane[p]
        g_full[me] = total
        moved = [send(g_full.at[me], g_full.at[me], si.at[n], ri.at[n], to[3]) for n, to in enumerate(beside)]
        for copy in moved:
            copy.wait()

        target = out if sweep == PASSES - 1 else panel
        gram = jnp.concatenate([g_full[p] for p in range(8)], 0)
        exchange_panel(place, normalised(own_t, gram), target, sp, rp, sq, rq)


def whole_call(lengths, block_subject, scans, panel):
    time_rows, cols = scans.shape
    rank = panel.shape[1]
    piece, quarter, rows = cols // 32, rank // 4, time_rows // 4
    return pl.pallas_call(
        whole_kernel,
        out_shape=jax.ShapeDtypeStruct((cols, rank), bf16),
        in_specs=[HBM, HBM, HBM, HBM],
        out_specs=VMEM,
        scratch_shapes=[
            pltpu.SMEM(lengths.shape, jnp.int32),
            pltpu.SMEM(block_subject.shape, jnp.int32),
            DMA((3,)),
            pltpu.VMEM((cols, rank), bf16),
            pltpu.VMEM((time_rows, cols), bf16),
            pltpu.VMEM((cols, rank), bf16),
            pltpu.VMEM((rank, piece), f32),
            pltpu.VMEM((4, rows, rank), f32),
            pltpu.VMEM((3, rows, rank), f32),
            pltpu.VMEM((4, rows, rank), bf16),
            pltpu.VMEM((4, 4, 4, quarter, piece), f32),
            pltpu.VMEM((4, 4, 4, quarter, piece), f32),
            pltpu.VMEM((4, 16, quarter, piece), f32),
            pltpu.VMEM((4, 16, quarter, piece), f32),
            pltpu.VMEM((8, rank // 8, rank), f32),
            pltpu.VMEM((7, rank // 8, rank), f32),
            pltpu.VMEM((16, rank // 8, rank), f32),
            pltpu.VMEM((8, rank // 8, rank), f32),
            DMA((8,)),
            *[DMA((3,))] * 4,
            *[DMA((4,))] * 2,
            DMA((4,)),
            DMA((4, 16)),
            *[DMA((7,))] * 2,
            *[DMA((16,))] * 2,
            *[DMA((7,))] * 2,
            DMA((4,)),
            DMA((4, 16)),
            *[DMA((1,))] * 2,
        ],
        compiler_params=pltpu.CompilerParams(
            collective_id=0, has_side_effects=True, vmem_limit_bytes=VMEM_BYTES
        ),
        name="range_finder",
    )(lengths, block_subject, scans, panel)


def on_device(scans, test_matrix, lengths, block_subject):
    lengths, block_subject, test_matrix = (
        pltpu.with_memory_space_constraint(a, pltpu.HBM) for a in (lengths, block_subject, test_matrix)
    )
    return whole_call(lengths, block_subject, scans, test_matrix).astype(f32)


def solution(mesh):
    placed = (P("subj", "vox"), P("vox", None), P(), P())
    return jax.shard_map(
        on_device, mesh=mesh, in_specs=placed, out_specs=P("vox", None), check_vma=False
    )
```

```python
import jax
import jax.numpy as jnp
from jax import lax
from jax.experimental import pallas as pl
from jax.experimental.pallas import tpu as pltpu
from jax.sharding import PartitionSpec as P

V = 49152
PASSES = 2
MESH = pl.DeviceIdType.MESH
VMEM_BYTES = 46 * 2**20
VMEM = pl.BlockSpec(memory_space=pltpu.VMEM)
HBM = pl.BlockSpec(memory_space=pltpu.HBM)
DMA = pltpu.SemaphoreType.DMA
f32, bf16 = jnp.float32, jnp.bfloat16
ORDERS = (("ya", "yb", "za", "zb"), ("yb", "ya", "zb", "za"), ("za", "zb", "ya", "yb"), ("zb", "za", "yb", "ya"))
WEIGHTS = (8, 4, 2, 1)


def flip_a(i):
    return i + 1 - 2 * lax.rem(i, 2)


def flip_b(i):
    return 3 - i


class Place:
    def __init__(self):
        here = lax.axis_index("subj")
        self.z, self.y, self.c = lax.div(here, 8), lax.rem(lax.div(here, 2), 4), lax.rem(here, 2)
        self.x = lax.axis_index("vox")

        self.zs = {(): self.z, ("za",): flip_a(self.z), ("zb",): flip_b(self.z)}
        self.zs["za", "zb"] = flip_b(self.zs[("za",)])
        self.ys = {(): self.y, ("ya",): flip_a(self.y), ("yb",): flip_b(self.y)}
        self.ys["ya", "yb"] = flip_b(self.ys[("ya",)])
        self.to = {
            bit: {"subj": (self.zs if bit[0] == "z" else self.ys)[(bit,)] * (8 if bit[0] == "z" else 2) + rest + self.c}
            for bit in ORDERS[0]
            for rest in [self.y * 2 if bit[0] == "z" else self.z * 8]
        }
        self.pairs = {
            zf + yf: z * 4 + y for zf, z in self.zs.items() for yf, y in self.ys.items()
        }
        self.beside_core = {"subj": here + 1 - 2 * self.c}

    def across(self, bit):
        return self.to[bit]

    def sibling(self):
        return self.beside_core

    def in_plane(self, step):
        z, y = lax.rem(self.z + step // 4, 4), lax.rem(self.y + step % 4, 4)
        return z * 4 + y, {"subj": z * 8 + y * 2 + self.c}

    def along_x(self, step, other_core):
        x = lax.rem(self.x + step, 4)
        c = 1 - self.c if other_core else self.c
        return x * 2 + c, {"subj": self.z * 8 + self.y * 2 + c, "vox": x}


def flips_of(order, m):
    flips = [bit for weight, bit in zip(WEIGHTS, order) if m & weight]
    return tuple(bit for bit in ("za", "zb", "ya", "yb") if bit in flips)


def pair_index(place, q, m):
    return place.pairs[flips_of(ORDERS[q], m)]


def greet(devices):
    barrier = pltpu.get_barrier_semaphore()
    for device in devices:
        pl.semaphore_signal(barrier, inc=1, device_id=device, device_id_type=MESH)
    return barrier, len(devices)


def send(src, dst, send_sem, recv_sem, device):
    copy = pltpu.make_async_remote_copy(
        src_ref=src, dst_ref=dst, send_sem=send_sem, recv_sem=recv_sem, device_id=device, device_id_type=MESH
    )
    copy.start()
    return copy


def landed(ref, sem):
    pltpu.make_async_copy(ref, ref, sem).wait()


def inverse_factor(gram):
    n, width = gram.shape[0], 8
    row, col = (lax.broadcasted_iota(jnp.int32, (n, n), d) for d in (0, 1))
    left, right = gram, (row == col).astype(jnp.float32)
    place = lax.broadcasted_iota(jnp.int32, (width, n), 0)
    done = []
    for k in range(0, n, width):
        columns = [jnp.broadcast_to(left[:, k + j : k + j + 1], left.shape) for j in range(width)]
        heads, tails = [c[:width] for c in columns], [c[width:] for c in columns]
        left_head, right_head = left[:width], right[:width]
        left, right = left[width:], right[width:]
        pivots = jnp.zeros((width, n), jnp.float32)
        for j in range(width):
            pivot = heads[j][j : j + 1]
            over = 1.0 / pivot
            pivots = jnp.where(place == j, jnp.broadcast_to(pivot, (width, n)), pivots)
            head = jnp.where(place > j, heads[j] * over, 0.0)
            left_row, right_row = left_head[j : j + 1], right_head[j : j + 1]
            if k + width < n:
                tail = tails[j] * over
                left, right = left - tail * left_row, right - tail * right_row
            for i in range(j + 1, width):
                factor = heads[j][i : i + 1]
                heads[i] = heads[i] - head * factor
                if k + width < n:
                    tails[i] = tails[i] - tail * factor
            left_head, right_head = left_head - head * left_row, right_head - head * right_row
        done.append(right_head * lax.rsqrt(pivots))
    return jnp.concatenate(done, 0)


def normalised(slice_t, gram):
    inverse = inverse_factor(gram / V)
    own = jnp.dot(inverse, slice_t[...], precision=lax.Precision.HIGHEST, preferred_element_type=f32)
    return own.T.astype(bf16)


def exchange_panel(place, own, panel, ss, rs, sc, rc):
    chunk = own.shape[0]
    size = chunk // 4

    def rows(core, pair, q=None):
        start = (core * 16 + pair) * chunk
        if q is None:
            return panel.at[pl.ds(pl.multiple_of(start, 32), chunk)]
        return panel.at[pl.ds(pl.multiple_of(start + q * size, 32), size)]

    def pass_on(q, m, weight):
        ref = rows(place.c, pair_index(place, q, m), q)
        device = {"subj": place.pairs[flips_of(ORDERS[q], weight)] * 2 + place.c}
        send(ref, ref, ss.at[q], rs.at[q, weight | m], device)

    rows(place.c, place.pairs[()])[...] = own
    for weight in (1, 2, 3, 4, 8):
        for q in range(4):
            pass_on(q, 0, weight)
    for m in range(16):
        for q in range(4):
            if m:
                landed(rows(place.c, pair_index(place, q, m), q), rs.at[q, m])
                for weight in (4, 8):
                    if weight > m:
                        pass_on(q, m, weight)
        for flips, pair in place.pairs.items():
            if m == max(sum(w for w, bit in zip(WEIGHTS, order) if bit in flips) for order in ORDERS):
                send(rows(place.c, pair), rows(place.c, pair), sc.at[0], rc.at[0], place.sibling())
    half = panel.at[pl.ds(0, 16 * chunk)]
    for q in range(4):
        landed(panel.at[pl.ds(0, 15 * size)], ss.at[q])
    landed(half, sc.at[0])
    landed(half, rc.at[0])


def whole_kernel(lengths_in, block_subject_in, scans, panel_in, out, *scratch):
    (
        lengths, block_subject, small_sem, first_panel, held, panel, own_t, part, got, full, away, arrived, mine, inbox, g_part, g_in, g_plane, g_full,
        load_sem, s1, r1, s2, r2, sc, rc, ss, rs, sg, rg, sh, rh, si, ri, sp, rp, sq, rq,
    ) = scratch
    place = Place()
    x = place.x
    rows = part.shape[1]
    rank, piece = own_t.shape
    quarter, width = rank // 4, 4 * piece
    owners = [lax.rem(x + step, 4) for step in (2, 1, 3, 0)]
    plane = [place.in_plane(step) for step in range(16)]
    beside = [(dx, dc, *place.along_x(dx, dc)) for dx in range(4) for dc in (0, 1) if dx or dc]
    greeted = greet([device for _, device in plane[1:]] + [device for *_, device in beside])

    def load(n):
        half = rows // 2
        at = pl.ds(pl.multiple_of(owners[n // 2] * rows + n % 2 * half, half), half)
        return pltpu.make_async_copy(scans.at[at], held.at[at], load_sem.at[n])

    small = [
        pltpu.make_async_copy(panel_in, first_panel, small_sem.at[0]),
        pltpu.make_async_copy(lengths_in, lengths, small_sem.at[1]),
        pltpu.make_async_copy(block_subject_in, block_subject, small_sem.at[2]),
    ]
    for copy in small:
        copy.start()
    ahead = 3
    for n in range(ahead):
        load(n).start()
    for copy in small:
        copy.wait()
    for sweep in range(PASSES):
        source = first_panel if sweep == 0 else panel
        copies = []
        for t in range(4):
            for n in (2 * t, 2 * t + 1):
                if sweep == 0 and n + ahead < 8:
                    load(n + ahead).start()
                if sweep == 0:
                    load(n).wait()

            own_rows = pl.ds(pl.multiple_of(owners[t] * rows, rows), rows)
            part[t] = jnp.dot(held[own_rows, :], source[...], preferred_element_type=f32)
            if t == 0 and sweep == 0:
                pl.semaphore_wait(*greeted)
            if t < 3:
                copies.append(send(part.at[t], got.at[t], s1.at[t], r1.at[t], {"vox": owners[t]}))
        total = part[3]
        for t in range(3):
            copies[t].wait()
            total = total + got[t]
        length = lengths[block_subject[lax.axis_index("subj")]]
        time_ids = x * rows + lax.broadcasted_iota(jnp.int32, total.shape, 0)
        full[x] = jnp.where(time_ids < length, total, f32(0.0)).astype(bf16)
        copies = [send(full.at[x], full.at[x], s2.at[t], r2.at[t], {"vox": owners[t]}) for t in range(3)]
        for copy in copies:
            copy.wait()
        left = jnp.concatenate([full[i] for i in range(4)], 0).T

        z_flips = (("za", "zb"), ("za",), ("zb",), ())
        z_far = [place.zs[flips] for flips in z_flips]
        core_copies = {}
        pair = [[pair_index(place, q, m) for m in range(16)] for q in range(4)]

        def pass_on(q, m):
            bit = ORDERS[q][4 - m.bit_length()]
            send(mine.at[q, pair[q][m]], inbox.at[q, m], ss.at[q], rs.at[q, m], place.across(bit))

        for away_side, k in ((1, 0), (1, 1), (0, 0), (1, 2), (0, 1), (1, 3), (0, 2), (0, 3)):
            core = 1 - place.c if away_side else place.c
            start = pl.multiple_of((core * 16 + z_far[k] * 4) * piece, width)
            block = jnp.dot(left, held[:, pl.ds(start, width)], preferred_element_type=f32)
            if not away_side:
                core_copies[k].wait()
            for y in range(4):
                for q in range(4):
                    value = block[q * quarter : (q + 1) * quarter, y * piece : (y + 1) * piece]
                    if away_side:
                        away[k, q, y] = value
                    else:
                        mine[q, z_far[k] * 4 + y] = value + arrived[k, q, y]
            if away_side:
                core_copies[k] = send(away.at[k], arrived.at[k], sc.at[k], rc.at[k], place.sibling())
                continue
            for m in range(15, 11, -1):
                for q in range(4):
                    if tuple(bit for bit in ("za", "zb") if bit in flips_of(ORDERS[q], m)) == z_flips[k]:
                        pass_on(q, m)

        for m in (7, 6, 5, 3, 4, 2, 1, 0):
            for q in range(4):
                value = mine[q, pair[q][m]]
                for weight in WEIGHTS:
                    if weight > m:
                        landed(inbox.at[q, weight | m], rs.at[q, weight | m])
                        value = value + inbox[q, weight | m]
                if m:
                    mine[q, pair[q][m]] = value
                    pass_on(q, m)
                    if m > 3:
                        pass_on(q, m + 4)
                else:
                    own_t[q * quarter : (q + 1) * quarter, :] = value

        own = own_t[...]
        gram = lax.dot_general(own, own, (((1,), (1,)), ((), ())), precision=lax.Precision.HIGHEST, preferred_element_type=f32)
        block = rank // 8
        for p in range(8):
            g_part[p] = gram[block * p : block * (p + 1)]
        me, here = x * 2 + place.c, plane[0][0]
        moved = [send(g_part.at[to[2]], g_in.at[n], sg.at[n], rg.at[n], to[3]) for n, to in enumerate(beside)]
        for q in range(4):
            landed(mine.at[q, pl.ds(0, 15)], ss.at[q])
        total = g_part[me]
        for n, copy in enumerate(moved):
            copy.wait()
            total = total + g_in[n]
        g_plane[here] = total
        moved = [send(g_plane.at[here], g_plane.at[here], sh.at[r], rh.at[r], plane[r][1]) for r in range(1, 16)]
        for copy in moved:
            copy.wait()
        total = g_plane[0]
        for p in range(1, 16):
            total = total + g_plane[p]
        g_full[me] = total
        moved = [send(g_full.at[me], g_full.at[me], si.at[n], ri.at[n], to[3]) for n, to in enumerate(beside)]
        for copy in moved:
            copy.wait()

        target = out if sweep == PASSES - 1 else panel
        gram = jnp.concatenate([g_full[p] for p in range(8)], 0)
        exchange_panel(place, normalised(own_t, gram), target, sp, rp, sq, rq)


def whole_call(lengths, block_subject, scans, panel):
    time_rows, cols = scans.shape
    rank = panel.shape[1]
    piece, quarter, rows = cols // 32, rank // 4, time_rows // 4
    return pl.pallas_call(
        whole_kernel,
        out_shape=jax.ShapeDtypeStruct((cols, rank), bf16),
        in_specs=[HBM, HBM, HBM, HBM],
        out_specs=VMEM,
        scratch_shapes=[
            pltpu.SMEM(lengths.shape, jnp.int32),
            pltpu.SMEM(block_subject.shape, jnp.int32),
            DMA((3,)),
            pltpu.VMEM((cols, rank), bf16),
            pltpu.VMEM((time_rows, cols), bf16),
            pltpu.VMEM((cols, rank), bf16),
            pltpu.VMEM((rank, piece), f32),
            pltpu.VMEM((4, rows, rank), f32),
            pltpu.VMEM((3, rows, rank), f32),
            pltpu.VMEM((4, rows, rank), bf16),
            pltpu.VMEM((4, 4, 4, quarter, piece), f32),
            pltpu.VMEM((4, 4, 4, quarter, piece), f32),
            pltpu.VMEM((4, 16, quarter, piece), f32),
            pltpu.VMEM((4, 16, quarter, piece), f32),
            pltpu.VMEM((8, rank // 8, rank), f32),
            pltpu.VMEM((7, rank // 8, rank), f32),
            pltpu.VMEM((16, rank // 8, rank), f32),
            pltpu.VMEM((8, rank // 8, rank), f32),
            DMA((8,)),
            *[DMA((3,))] * 4,
            *[DMA((4,))] * 2,
            DMA((4,)),
            DMA((4, 16)),
            *[DMA((7,))] * 2,
            *[DMA((16,))] * 2,
            *[DMA((7,))] * 2,
            DMA((4,)),
            DMA((4, 16)),
            *[DMA((1,))] * 2,
        ],
        compiler_params=pltpu.CompilerParams(
            collective_id=0, has_side_effects=True, vmem_limit_bytes=VMEM_BYTES
        ),
        name="range_finder",
    )(lengths, block_subject, scans, panel)


def on_device(scans, test_matrix, lengths, block_subject):
    lengths, block_subject, test_matrix = (
        pltpu.with_memory_space_constraint(a, pltpu.HBM) for a in (lengths, block_subject, test_matrix)
    )
    return whole_call(lengths, block_subject, scans, test_matrix).astype(f32)


def solution(mesh):
    placed = (P("subj", "vox"), P("vox", None), P(), P())
    return jax.shard_map(
        on_device, mesh=mesh, in_specs=placed, out_specs=P("vox", None), check_vma=False
    )
```
